256 devices in a mesh: prow: 2 (over core), pcol: 128 (over z, y, x).
Axes of the slice: x: 4, y: 4, z: 8, core: 2. Of those that a mesh axis runs over, the one named last changes fastest.
Arguments:
- matrix: float32 [8192, 49152], P('prow', 'pcol'), may hold values from -8 to 8, as said below
- pivot_rows: int32 [128], replicated, may hold values from 0 to 8191, as said below
Outputs:
- factored: float32 [8192, 49152], P('prow', 'pcol')
The draws below stay inside these ranges and needn't reach their ends.
Inputs may be any that keep to these rules, and one draw needn't show every extreme that they name: `pivot_rows`: 128 distinct row indices; exactly 32 of them are below 128. `matrix`: in row pivot_rows[k] the entry of column k has magnitude 4 or more and the other entries of the first 128 columns have magnitude 0.3 or less; the LU factorization without row exchanges of the pivot block has all its diagonal entries of magnitude 1 or more.
All inputs are finite; a program needn't handle non-finite values.
Results may differ from the reference program's by a relative error of at most 0.0003.
Values may be sent and summed in bfloat16 or wider, within the bound.
A program may use at most 128 MiB of HBM per device.

```python
import jax
import jax.numpy as jnp
from jax import lax

NB = 128
ORDER = 8192
COLS = 49152


def pick_rows(key):
    base_key = jax.random.fold_in(key, 11)
    first_key, second_key, third_key = jax.random.split(base_key, 3)
    few_top = NB // 4
    top_rows = jax.random.permutation(first_key, NB)[:few_top]
    other_rows = jax.random.permutation(second_key, ORDER - NB)[:NB - few_top] + NB
    joined = jnp.concatenate([top_rows, other_rows]).astype(jnp.int32)
    return jax.random.permutation(third_key, joined).astype(jnp.int32)


def draw_pivot_rows(key, part):
    return pick_rows(key)


def draw_matrix(key, part):
    chosen_rows = pick_rows(key)
    keys = jax.random.split(jax.random.fold_in(key, 23), 4)
    background = jax.random.truncated_normal(keys[0], -6.0, 6.0, (ORDER, COLS), jnp.float32)
    magnitude = jnp.exp(jax.random.uniform(keys[2], (NB,), jnp.float32, jnp.log(4.0), jnp.log(8.0)))
    offdiag = jax.random.uniform(keys[1], (NB, NB), jnp.float32, -0.3, 0.3)
    signs = jnp.where(jax.random.bernoulli(keys[3], 0.5, (NB,)), 1.0, -1.0).astype(jnp.float32)
    eye_mat = jnp.eye(NB, dtype=jnp.float32)
    block = offdiag * (1.0 - eye_mat) + eye_mat * (signs * magnitude)[:, None]
    return background.at[chosen_rows, :NB].set(block).astype(jnp.float32)


def setup_inputs(seed: int = 0) -> dict:
    arg_keys = jax.random.split(jax.random.key(seed), 3)
    return {
        "matrix": draw_matrix(jax.random.fold_in(arg_keys[2], 71), 0),
        "pivot_rows": draw_pivot_rows(jax.random.fold_in(arg_keys[2], 71), 0),
    }


def small_factor(block):
    length = block.shape[0]
    for column in range(length - 1):
        factor_col = block[column + 1:, column] / block[column, column]
        block = block.at[column + 1:, column].set(factor_col)
        block = block.at[column + 1:, column + 1:].add(-factor_col[:, None] * block[column, column + 1:][None, :])
    return block

def factor(block):
    length = block.shape[0]
    if length <= 16:
        return small_factor(block)
    middle = length // 2
    top = factor(block[:middle, :middle])
    unit_low = jnp.tril(top, -1) + jnp.eye(middle, dtype=block.dtype)
    up_tri = jnp.triu(top)
    right_part = jax.scipy.linalg.solve_triangular(unit_low, block[:middle, middle:], lower=True, unit_diagonal=True)
    down_part = jax.scipy.linalg.solve_triangular(up_tri, block[middle:, :middle].T, trans=1, lower=False).T
    schur = block[middle:, middle:] - jnp.dot(down_part, right_part, precision=lax.Precision.HIGHEST)
    bottom = factor(schur)
    return jnp.concatenate([jnp.concatenate([top, right_part], 1), jnp.concatenate([down_part, bottom], 1)], 0)

def swap_lists(pivot_rows):
    ladder = jnp.arange(NB, dtype=jnp.int32)
    sentinel = jnp.int32(2 ** 30)
    chosen = jnp.any(pivot_rows[:, None] == ladder[None, :], axis=0)
    displaced = jnp.sort(jnp.where(chosen, sentinel, ladder))
    landing = jnp.sort(jnp.where(pivot_rows >= NB, pivot_rows, sentinel))
    return (landing, displaced)

def split_three(source):
    first = source.astype(jnp.bfloat16)
    rest = source - lax.optimization_barrier(first).astype(source.dtype)
    second = rest.astype(jnp.bfloat16)
    third = (rest - lax.optimization_barrier(second).astype(source.dtype)).astype(jnp.bfloat16)
    return (first, second, third)

def reference(matrix, pivot_rows):
    landing, displaced = swap_lists(pivot_rows)
    targets = jnp.concatenate([jnp.arange(NB, dtype=jnp.int32), landing]).astype(jnp.int32)
    sources = jnp.concatenate([pivot_rows, jnp.minimum(displaced, NB - 1)]).astype(jnp.int32)
    swapped = matrix.at[targets].set(matrix[sources], mode='drop')
    packed = factor(swapped[:NB, :NB])
    diag_lower = jnp.tril(packed, -1) + jnp.eye(NB, dtype=packed.dtype)
    diag_upper = jnp.triu(packed)
    upper = jax.scipy.linalg.solve_triangular(diag_lower, swapped[:NB, NB:], lower=True, unit_diagonal=True)
    lower = jax.scipy.linalg.solve_triangular(diag_upper, swapped[NB:, :NB].T, trans=1, lower=False).T
    lower_slices = split_three(lower)
    upper_slices = split_three(upper)
    left_stack = jnp.concatenate([lower_slices[i] for i in (0, 0, 0, 1, 1, 1, 2, 2, 2)], axis=1).astype(jnp.float32)
    right_stack = jnp.concatenate([upper_slices[j] for j in (0, 1, 2, 0, 1, 2, 0, 1, 2)], axis=0).astype(jnp.float32)
    update = jnp.dot(left_stack, right_stack, precision=lax.Precision.HIGHEST)
    head = jnp.concatenate([packed, upper], 1)
    tail = jnp.concatenate([lower, swapped[NB:, NB:] - update], 1)
    return jnp.concatenate([head, tail], 0)
```

```python
import functools

import jax
import jax.numpy as jnp
from jax import lax
from jax.experimental import pallas as pl
from jax.experimental.pallas import tpu as pltpu
from jax.sharding import PartitionSpec as P

NB = 128
FEW = 96
F32 = jnp.float32
BF16 = jnp.bfloat16
I32 = jnp.int32
HIGH = lax.Precision.HIGHEST
MESH = pl.DeviceIdType.MESH

TREES_A = (
    4196353, 201523325, 268626057, 201455808, 124977344, 180617363, 230918337, 144870656,
    174326016, 239403250, 289687809, 205753664, 201523392, 268697770, 335759561, 268592384,
    201523392, 268697755, 335763673, 268588288, 166985984, 226820307, 277104897, 209917248,
    208994624, 289800451, 356845905, 272893312, 268697856, 335872194, 402917649, 335742272,
    268697856, 335872218, 402942229, 335770944, 233111872, 278266134, 361056577, 293868928,
    291897728, 340197714, 407243137, 340069824, 335872320, 403046658, 470108481, 402916736,
    335872320, 403046682, 470108493, 402945408, 295043456, 348586306, 411457941, 344282560,
    359072192, 408420754, 474417617, 407242240, 403046784, 470221122, 537282961, 470107584,
    403046784, 478609735, 545655169, 604308928, 344392128, 412615042, 482806209, 545654272,
    409469440, 470352322, 537397761, 482807360, 470221248, 537395586, 604441025, 537273856,
    335872320, 403046671, 470092097, 402926976, 279314816, 383189315, 411441537, 344266176,
    340197824, 440926594, 474417601, 409339392, 403046784, 470221155, 537266561, 470093248,
    268697856, 335872231, 402917653, 335789392, 247791936, 311820546, 344295749, 281320832,
    307626368, 341246306, 407243169, 373624256, 335872320, 403046658, 470092097, 402918784,
    201523392, 268697766, 335751488, 268608896, 178520320, 244646083, 277088513, 247661888,
    205848896, 274071843, 340068673, 272895360, 268697856, 335872227, 402917665, 335742272,
)
TREES_B = (
    33570824, 201523392, 268697856, 201523392, 201523392, 268697856, 335872320, 268697856,
    268697770, 335872200, 403046664, 335872202, 201523323, 268697788, 335872228, 268697766,
    469859520, 538083584, 604217664, 537049344, 537036032, 604210496, 671388032, 604209472,
    604210394, 671383832, 738558280, 671400200, 537044126, 604225741, 671400204, 604217540,
    436370688, 503517504, 537137536, 503515456, 503519552, 570708352, 637862336, 570687872,
    570687752, 637862217, 705036696, 637878600, 503515351, 570687765, 637870404, 570687756,
    369327424, 436479360, 503656896, 436470144, 436476288, 503648704, 570819072, 503644608,
    503644488, 570835336, 637993416, 570835336, 436488478, 503660893, 570827140, 503644492,
    306470272, 373637568, 440812160, 373639616, 369446336, 436617728, 503792200, 436619776,
    438714760, 503792072, 570966540, 503794120, 370501964, 446054796, 512180800, 436619660,
    250954048, 303448448, 369574336, 310788480, 275136896, 336019904, 403194368, 338117056,
    372719946, 404242825, 470368744, 403194248, 302399759, 336019789, 403194244, 371671396,
    183910656, 210190656, 268976512, 203882816, 208093504, 307773824, 336150976, 268976512,
    271073546, 336150856, 403325320, 336150856, 203899110, 303579405, 344539468, 268976388,
    116850880, 152568064, 218694976, 164233472, 152568064, 256442688, 290062720, 220791104,
    218693864, 285868296, 353042760, 285868296, 160956580, 219742444, 285868300, 227082444,
)
DEEPEST = 11

TREES = 6
CHUNKS = 8
PIECE = 88
SPAN = PIECE * CHUNKS
TAIL = 48
EXT = 4096
INV = TREES * SPAN
HELD = INV + TREES * TAIL


def swap_lists(pivot_col, pivot_row, row_start, tab_ref):
    lane = lax.broadcasted_iota(I32, (NB, NB), 1)
    sub = lax.broadcasted_iota(I32, (NB, NB), 0)
    low = pivot_col >= NB
    smaller = (pivot_row < pivot_col) & (pivot_row >= NB)
    rank = jnp.sum(jnp.where(smaller, 1.0, 0.0), axis=1, keepdims=True)
    lane_f = lane.astype(F32)
    hit = (rank == lane_f) & low
    landing = jnp.sum(jnp.where(hit, pivot_col.astype(F32), 0.0), axis=0, keepdims=True)
    chosen = jnp.sum(jnp.where(pivot_col == lane, 1.0, 0.0), axis=0, keepdims=True)
    free = jnp.broadcast_to(1.0 - chosen, (NB, NB))
    ahead = jnp.sum(jnp.where(lane < sub, free, 0.0), axis=1, keepdims=True)
    own = jnp.sum(jnp.where(lane == sub, free, 0.0), axis=1, keepdims=True)
    place = (ahead == lane_f) & (own > 0.5)
    displaced = jnp.sum(jnp.where(place, sub.astype(F32), 0.0), axis=0, keepdims=True)
    bound = row_start + lane * TILE
    starts = jnp.sum(jnp.where(low & (pivot_col < bound), 1.0, 0.0), axis=0, keepdims=True)
    tab_ref[...] = jnp.concatenate(
        [landing, displaced, starts, jnp.zeros((5, NB), F32)], axis=0
    ).astype(I32)


def gather_kernel(pivots_sm, pivots_v, matrix, rows_ref, mask_ref, tab_ref, tab_sm, sems):
    rows_dev = matrix.shape[0]
    row_start = lax.axis_index("prow") * rows_dev

    def fetch(source, k):
        local = jnp.clip(source - row_start, 0, rows_dev - 1)
        pltpu.make_async_copy(
            matrix.at[pl.ds(local, 1), :], rows_ref.at[pl.ds(k, 1), :], sems.at[0]
        ).start()

    def first(i, carry):
        for j in range(8):
            k = 8 * i + j
            fetch(pivots_sm[k], k)
        return carry

    lax.fori_loop(0, NB // 8, first, 0)
    pivot_row = jnp.broadcast_to(pivots_v[...], (NB, NB))
    pivot_col = jnp.transpose(pivot_row.astype(F32)).astype(I32)
    swap_lists(pivot_col, pivot_row, row_start, tab_ref)
    move = pltpu.make_async_copy(tab_ref, tab_sm, sems.at[1])
    move.start()
    inside = (pivot_col >= row_start) & (pivot_col < row_start + rows_dev)
    mask_ref[...] = jnp.where(inside, 1.0, 0.0)
    move.wait()

    def second(i, carry):
        for j in range(8):
            k = 8 * i + j
            fetch(tab_sm[1, k], NB + k)
        return carry

    lax.fori_loop(0, FEW // 8, second, 0)
    pltpu.make_async_copy(
        matrix.at[pl.ds(0, NB + FEW), :], rows_ref, sems.at[0]
    ).wait()


def gather(matrix, pivot_rows):
    cols = matrix.shape[1]
    return pl.pallas_call(
        gather_kernel,
        name="gather_rows",
        out_shape=(
            jax.ShapeDtypeStruct((NB + FEW, cols), F32),
            jax.ShapeDtypeStruct((NB, NB), F32),
            jax.ShapeDtypeStruct((8, NB), I32),
        ),
        in_specs=[
            pl.BlockSpec(memory_space=pltpu.SMEM),
            pl.BlockSpec(memory_space=pltpu.VMEM),
            pl.BlockSpec(memory_space=pl.ANY),
        ],
        out_specs=(pl.BlockSpec(memory_space=pltpu.VMEM),) * 3,
        scratch_shapes=[pltpu.SMEM((8, NB), I32), pltpu.SemaphoreType.DMA((2,))],
    )(pivot_rows, pivot_rows.reshape(1, NB), matrix)


def pick(values, bits):
    while len(values) > 1:
        bit, bits = bits[0], bits[1:]
        values = [
            lo if isinstance(lo, int) and lo == hi else jnp.where(bit, hi, lo)
            for lo, hi in zip(values[::2], values[1::2])
        ]
    return values[0]


def eliminate(block, packed_ref, linv_ref, binv_ref, upper_ref, scale_ref):
    lane = lax.broadcasted_iota(I32, (8, NB), 1)
    sub = lax.broadcasted_iota(I32, (8, NB), 0)
    groups = NB // 8
    left = tuple(block[8 * q : 8 * q + 8, :] for q in range(groups))
    right = tuple(jnp.where(lane == sub + 8 * q, 1.0, 0.0) for q in range(groups))

    def row_of(x, k):
        return jnp.broadcast_to(x[k : k + 1, :], (8, NB))

    def column_of(x, k):
        return jnp.broadcast_to(x[:, k : k + 1], (8, NB))

    def turn(g, carry):
        a, z = list(carry[0]), list(carry[1])
        active = lane < NB - 8 * g
        upper, linv, scale = a[0], z[0], jnp.zeros((8, NB), F32)
        column = [column_of(a[0], j) for j in range(8)]
        for k in range(8):
            pivot = row_of(column[k], k)
            row_a, row_z = row_of(a[0], k), row_of(z[0], k)
            inverse = 1.0 / pivot
            here = sub == k
            upper = jnp.where(here, row_a, upper)
            linv = jnp.where(here, row_z, linv)
            scale = jnp.where(here, inverse, scale)
            row_a = jnp.where(
                lane > k, jnp.where(active, row_a, 0.0), jnp.where(lane == k, pivot - 1.0, 0.0)
            )
            first = jnp.where(here, 0.0, column[k] * inverse)
            for j in range(k + 1, 8):
                column[j] = column[j] - first * row_of(column[j], k)
            for q in range(groups):
                factor = first if q == 0 else column_of(a[q], k) * inverse
                a[q] = a[q] - factor * row_a
                z[q] = z[q] - factor * row_z
        at = pl.ds(pl.multiple_of(8 * g, 8), 8)
        upper_ref[at, :] = upper
        linv_ref[at, :] = linv
        scale_ref[at, :] = scale
        a = [pltpu.roll(x, NB - 8, 1) for x in a]
        return tuple(a[1:] + a[:1]), tuple(z[1:] + z[:1])

    left, right = lax.fori_loop(0, groups, turn, (left, right))
    for q in range(groups):
        at = slice(8 * q, 8 * q + 8)
        upper = upper_ref[at, :]
        if q:
            upper = pltpu.roll(upper, 8 * q, 1)
        packed_ref[at, :] = jnp.where(lane < sub + 8 * q, left[q], upper)
        binv_ref[at, :] = right[q] * scale_ref[at, :]


def exchange_kernel(
    matrix, rows_ref, mask_ref, held, incoming_ref, returning_ref, packed_ref,
    other, upper_ref, scale_ref, arrive, depart, swap_sems,
):
    plane, chip = lax.axis_index("prow"), lax.axis_index("pcol")
    x, y, z = chip % 4, (chip // 4) % 4, chip // 16
    place = jnp.where(plane == 0, chip, (4 - x) % 4 + 4 * ((4 - y) % 4) + 16 * ((8 - z) % 8))
    bits = [(place // (2**i)) % 2 == 1 for i in range(7)]
    words = [pick(list(table), bits) for table in (TREES_A, TREES_B)]
    nodes = [(words[t // 3] // (2 ** (10 * (t % 3)))) % 1024 for t in range(TREES)]
    sends = [node % 64 for node in nodes]
    depths = [node // 64 for node in nodes]
    step = 1 - 2 * plane
    neighbours = []
    for sign in (step, -step):
        neighbours.append((
            (x + sign + 4) % 4 + 4 * y + 16 * z,
            x + 4 * ((y + sign + 4) % 4) + 16 * z,
            x + 4 * y + 16 * ((z + sign + 8) % 8),
        ))
    neighbours = [neighbours[d % 2][d // 2] for d in range(6)]
    root = chip == 0

    barrier = pltpu.get_barrier_semaphore()
    for there in neighbours:
        pl.semaphore_signal(barrier, inc=1, device_id=(plane, there), device_id_type=MESH)
    pl.semaphore_signal(barrier, inc=1, device_id=(1 - plane, chip), device_id_type=MESH)
    pl.semaphore_wait(barrier, 7)

    swap = pltpu.make_async_remote_copy(
        src_ref=rows_ref, dst_ref=other, send_sem=swap_sems.at[0], recv_sem=swap_sems.at[1],
        device_id=(1 - plane, chip), device_id_type=MESH,
    )
    swap.start()

    def piece(t, c):
        return pl.ds(pl.multiple_of(t * SPAN + c * PIECE, 8), PIECE)

    @pl.when(root)
    def _():
        for c in range(CHUNKS):
            for t in range(TREES):
                lo = t * SPAN + c * PIECE
                size = min(PIECE, EXT - lo)
                if size > 0:
                    pltpu.make_async_copy(
                        matrix.at[pl.ds(lo, size), pl.ds(0, NB)],
                        held.at[pl.ds(lo, size), :],
                        arrive.at[t, c],
                    ).start()

    def send(t, c, at):
        for d in range(6):
            @pl.when((sends[t] // (2**d)) % 2 == 1)
            def _():
                pltpu.make_async_remote_copy(
                    src_ref=held.at[at, :], dst_ref=held.at[at, :],
                    send_sem=depart.at[t, d], recv_sem=arrive.at[t, c],
                    device_id=(plane, neighbours[d]), device_id_type=MESH,
                ).start()

    def arrived(t, c, at):
        pltpu.make_async_copy(held.at[at, :], held.at[at, :], arrive.at[t, c]).wait()

    late = CHUNKS - 2

    def pass_on(s, carry):
        for t in range(TREES):
            c = s - depths[t]
            limit = CHUNKS
            if t == TREES - 1:
                limit = jnp.where(root, late, CHUNKS)

            @pl.when((c >= 0) & (c < limit))
            def _():
                at = piece(t, c)
                arrived(t, c, at)
                send(t, c, at)
        return carry

    lax.fori_loop(0, jnp.where(root, CHUNKS, DEEPEST + CHUNKS), pass_on, 0)

    swap.wait()
    mine = jnp.concatenate([mask_ref[...]] * (matrix.shape[1] // NB), axis=1) > 0.5
    incoming_ref[...] = jnp.where(mine, rows_ref[:NB, :], other[:NB, :])
    returning_ref[...] = jnp.where(plane == 0, rows_ref[NB:, :], other[NB:, :])

    @pl.when(root)
    def _():
        t, lo = TREES - 1, (TREES - 1) * SPAN + late * PIECE
        part = pl.ds(lo, EXT - lo)
        pltpu.make_async_copy(held.at[part, :], held.at[part, :], arrive.at[t, late]).wait()
        held[EXT : EXT + FEW, :] = returning_ref[:, :NB]
        held[EXT + FEW : INV, :] = jnp.zeros((INV - EXT - FEW, NB), F32)
        for c in range(late, CHUNKS):
            send(t, c, pl.ds(t * SPAN + c * PIECE, PIECE))
        eliminate(
            incoming_ref[:, :NB], packed_ref,
            held.at[INV : INV + NB, :], held.at[INV + NB : INV + 2 * NB, :],
            upper_ref, scale_ref,
        )
        held[INV + 2 * NB : HELD, :] = jnp.zeros((HELD - INV - 2 * NB, NB), F32)

    def pass_tail(s, carry):
        for t in range(TREES):
            @pl.when(depths[t] == s)
            def _():
                at = pl.ds(INV + t * TAIL, TAIL)

                @pl.when(s > 0)
                def _():
                    arrived(t, CHUNKS, at)
                send(t, CHUNKS, at)
        return carry

    lax.fori_loop(0, jnp.where(root, 1, DEEPEST + 1), pass_tail, 0)

    for t in range(TREES):
        for d in range(6):
            @pl.when((sends[t] // (2**d)) % 2 == 1)
            def _():
                at = pl.ds(0, SPAN + TAIL)
                pltpu.make_async_copy(held.at[at, :], held.at[at, :], depart.at[t, d]).wait()


def exchange(matrix, rows, mask):
    cols = matrix.shape[1]
    vmem = pl.BlockSpec(memory_space=pltpu.VMEM)
    return pl.pallas_call(
        exchange_kernel,
        name="exchange",
        out_shape=(
            jax.ShapeDtypeStruct((HELD, NB), F32),
            jax.ShapeDtypeStruct((NB, cols), F32),
            jax.ShapeDtypeStruct((FEW, cols), F32),
            jax.ShapeDtypeStruct((NB, NB), F32),
        ),
        in_specs=[pl.BlockSpec(memory_space=pl.ANY), vmem, vmem],
        out_specs=(vmem,) * 4,
        scratch_shapes=[
            pltpu.VMEM((NB + FEW, cols), F32),
            pltpu.VMEM((NB, NB), F32),
            pltpu.VMEM((NB, NB), F32),
            pltpu.SemaphoreType.DMA((TREES, CHUNKS + 1)),
            pltpu.SemaphoreType.DMA((TREES, 6)),
            pltpu.SemaphoreType.DMA((2,)),
        ],
        compiler_params=pltpu.CompilerParams(
            collective_id=0, has_side_effects=True, vmem_limit_bytes=24 * 2**20
        ),
    )(matrix, rows, mask)


TILE = 512


def update_kernel(
    tab, tile_ref, panel_ref, ext_ref, linv_ref, binv_ref, incoming_ref, returning_ref, packed_ref, out_ref,
    right, patch, top,
):
    j = pl.program_id(0)
    plane, first = lax.axis_index("prow"), lax.axis_index("pcol") == 0

    def product(left_f32):
        high = left_f32.astype(BF16)
        low = (left_f32 - high.astype(F32)).astype(BF16)
        return jnp.dot(
            jnp.concatenate([high, high, low], axis=1), right[...], preferred_element_type=F32
        )

    def keep(block):
        return jnp.concatenate([jnp.where(first, 0.0, block[:, :NB]), block[:, NB:]], axis=1)

    @pl.when(j == 0)
    def _():
        source = incoming_ref[...]
        top[...] = jnp.dot(linv_ref[...], source, precision=HIGH, preferred_element_type=F32)
        lane = lax.broadcasted_iota(I32, (NB, NB), 1)
        sub = lax.broadcasted_iota(I32, (NB, NB), 0)
        packed = packed_ref[...]
        unit = jnp.where(lane < sub, packed, jnp.where(lane == sub, 1.0, 0.0))

        @pl.when(first)
        def _():
            top[:, :NB] = packed
        source = jnp.concatenate([jnp.where(first, -unit, source[:, :NB]), source[:, NB:]], axis=1)
        w = jnp.dot(binv_ref[...], source, precision=HIGH, preferred_element_type=F32)
        high = w.astype(BF16)
        right[0:NB, :] = high
        right[NB : 2 * NB, :] = (w - high.astype(F32)).astype(BF16)
        right[2 * NB :, :] = high
        patch[...] = keep(returning_ref[...]) - product(ext_ref[0:FEW, :])

    out_ref[...] = keep(tile_ref[...]) - product(panel_ref[...])

    @pl.when((j == 0) & (plane == 0))
    def _():
        out_ref[0:NB, :] = top[...]

    base = plane * 4096 + j * TILE

    def land(i, carry):
        out_ref[pl.ds(tab[0, i] - base, 1), :] = patch[pl.ds(i, 1), :]
        return carry

    lax.fori_loop(tab[2, j], tab[2, j + 1], land, 0)


def update(matrix, held, incoming, returning, packed, tab):
    rows, cols = matrix.shape
    vmem = pl.BlockSpec(memory_space=pltpu.VMEM)
    whole = lambda shape: pl.BlockSpec(shape, lambda j: (0, 0))
    return pl.pallas_call(
        update_kernel,
        name="update",
        grid=(rows // TILE,),
        out_shape=jax.ShapeDtypeStruct((rows, cols), F32),
        in_specs=[
            pl.BlockSpec(memory_space=pltpu.SMEM),
            pl.BlockSpec((TILE, cols), lambda j: (j, 0)),
            pl.BlockSpec((TILE, NB), lambda j: (j, 0)),
            pl.BlockSpec((NB, NB), lambda j: (EXT // NB, 0)),
            pl.BlockSpec((NB, NB), lambda j: (INV // NB, 0)),
            pl.BlockSpec((NB, NB), lambda j: (INV // NB + 1, 0)),
            whole((NB, cols)), whole((FEW, cols)), whole((NB, NB)),
        ],
        out_specs=pl.BlockSpec((TILE, cols), lambda j: (j, 0)),
        scratch_shapes=[
            pltpu.VMEM((3 * NB, cols), BF16),
            pltpu.VMEM((FEW, cols), F32),
            pltpu.VMEM((NB, cols), F32),
        ],
        compiler_params=pltpu.CompilerParams(vmem_limit_bytes=24 * 2**20),
    )(tab, matrix, held, held, held, held, incoming, returning, packed)


def on_device(matrix, pivot_rows):
    rows, mask, tab = gather(matrix, pivot_rows)
    held, incoming, returning, packed = exchange(matrix, rows, mask)
    return update(matrix, held, incoming, returning, packed, tab)


def solution(mesh):
    return jax.shard_map(
        on_device, mesh=mesh, in_specs=(P("prow", "pcol"), P()), out_specs=P("prow", "pcol"), check_vma=False
    )
```

```python
import functools

import jax
import jax.numpy as jnp
from jax import lax
from jax.experimental import pallas as pl
from jax.experimental.pallas import tpu as pltpu
from jax.sharding import PartitionSpec as P

NB = 128
FEW = 96
F32 = jnp.float32
BF16 = jnp.bfloat16
I32 = jnp.int32
HIGH = lax.Precision.HIGHEST
MESH = pl.DeviceIdType.MESH

HOPS = (
    (1, 0, 0), (3, 0, 0), (2, 0, 0), (0, 1, 0), (0, 3, 0), (0, 2, 0),
    (0, 0, 1), (0, 0, 7), (0, 0, 2), (0, 0, 6), (0, 0, 3), (0, 0, 5), (0, 0, 4),
)
PANEL_TREES = (
    (
        768, 0, 0, 0, 0, 0, 0, 0, 0, 0,
        0, 0, 0, 0, 0, 98313, 49160, 73745, 90240, 0,
        73737, 90241, 0, 90264, 90240, 98433, 0, 0, 73730, 90240,
        0, 90114, 24723, 49337, 73744, 49224, 0, 0, 90184, 73923,
        0, 73920, 0, 0, 49298, 73792, 0, 74320, 0, 0,
        0, 73731, 0, 0, 0, 90177, 0, 98323, 0, 0,
        0, 90178, 0, 90194, 0, 90242, 98305, 0, 0, 0,
        0, 0, 98312, 0, 0, 0, 0, 0, 0, 0,
        49155, 73864, 73880, 0, 98432, 90240, 98432, 0, 73881, 98440,
        0, 98448, 0, 0, 98449, 0, 24804, 0, 57592, 0,
        0, 0, 73795, 98320, 57547, 0, 82688, 73920, 0, 98312,
        73795, 0, 49169, 73800, 73729, 0, 98496, 0, 98377, 0,
        73745, 0, 0, 98368, 0, 0, 98371, 0,
    ),
    (
        264, 0, 0, 0, 26757, 0, 49736, 0, 0, 90120,
        73738, 0, 0, 0, 90120, 0, 49169, 73880, 90176, 0,
        0, 0, 73852, 0, 90240, 0, 90176, 98432, 73872, 0,
        0, 90240, 24963, 49160, 0, 49328, 0, 73802, 0, 98432,
        0, 90248, 0, 73937, 0, 0, 90176, 73859, 73752, 0,
        0, 98306, 0, 90137, 0, 0, 0, 0, 0, 98323,
        0, 0, 0, 0, 57502, 0, 81952, 73872, 73729, 98305,
        0, 0, 0, 0, 0, 0, 73793, 98520, 0, 98434,
        73793, 0, 0, 0, 57375, 0, 81968, 73880, 73921, 98305,
        0, 98432, 98370, 0, 0, 0, 0, 0, 98306, 0,
        0, 98306, 73818, 90128, 0, 0, 98313, 0, 0, 0,
        0, 0, 65537, 90113, 0, 90176, 41011, 65544, 0, 65752,
        0, 90241, 0, 90113, 73731, 90241, 0, 90240,
    ),
    (
        17, 25608, 0, 0, 0, 45257, 65553, 90128, 0, 65537,
        0, 65601, 27143, 0, 53312, 41360, 0, 0, 90114, 0,
        90264, 65611, 0, 0, 0, 90113, 0, 90128, 0, 0,
        73803, 90121, 0, 0, 0, 90115, 0, 90115, 0, 0,
        0, 0, 0, 90131, 0, 0, 90114, 73816, 0, 57496,
        0, 0, 98306, 73739, 98320, 0, 0, 98432, 0, 0,
        98456, 73729, 98320, 90136, 0, 0, 0, 0, 0, 81940,
        0, 0, 98306, 0, 0, 0, 73880, 0, 90171, 0,
        73730, 0, 0, 98432, 98432, 0, 0, 0, 73746, 98448,
        0, 98320, 57497, 73816, 98329, 0, 0, 0, 98305, 0,
        90114, 90113, 0, 0, 73746, 0, 98368, 0, 49244, 98328,
        73881, 0, 0, 90129, 0, 0, 0, 65691, 90624, 0,
        0, 0, 0, 90129, 73736, 0, 0, 65562,
    ),
    (
        2049, 24625, 41160, 0, 0, 0, 65793, 90192, 73744, 49619,
        73921, 90120, 65600, 41218, 0, 0, 0, 0, 65561, 0,
        0, 90128, 0, 0, 90128, 73746, 90113, 0, 90121, 0,
        90241, 0, 0, 0, 0, 0, 0, 98320, 90177, 0,
        98320, 73811, 98369, 0, 90120, 73795, 90121, 0, 0, 0,
        0, 98432, 0, 0, 0, 0, 0, 98306, 0, 0,
        0, 90123, 0, 0, 57474, 0, 98496, 73930, 73864, 98456,
        0, 98442, 98312, 0, 0, 0, 0, 98305, 0, 98432,
        33016, 0, 0, 0, 57539, 73936, 0, 73792, 57414, 0,
        90320, 82496, 57411, 73937, 0, 73920, 57346, 0, 90120, 73792,
        73792, 0, 0, 98368, 0, 0, 0, 0, 73792, 98329,
        0, 0, 0, 90130, 65682, 0, 0, 90113, 0, 0,
        0, 73746, 90113, 0, 0, 0, 90113, 0,
    ),
    (
        545, 25808, 0, 0, 0, 0, 73792, 73793, 24838, 0,
        59536, 49168, 0, 40977, 65537, 90120, 0, 40979, 65680, 0,
        0, 0, 98312, 90129, 0, 90128, 0, 98312, 90240, 65554,
        0, 0, 0, 73739, 98305, 0, 0, 0, 0, 98368,
        57538, 0, 98322, 73946, 0, 98307, 0, 0, 0, 57563,
        73809, 0, 98432, 73729, 0, 0, 73744, 0, 0, 0,
        0, 73872, 98321, 0, 0, 73738, 98320, 0, 0, 98376,
        0, 98395, 0, 0, 0, 0, 90258, 0, 0, 0,
        90114, 0, 0, 0, 73744, 0, 0, 0, 0, 0,
        90259, 0, 73873, 90249, 0, 0, 24600, 65537, 90256, 0,
        49283, 0, 0, 74264, 73792, 0, 98322, 0, 49299, 0,
        0, 73920, 65546, 41098, 0, 0, 0, 65600, 98320, 0,
        0, 98312, 73883, 98320, 0, 0, 0, 90113,
    ),
    (
        34, 65544, 40978, 27658, 0, 90120, 0, 41153, 28864, 0,
        0, 90240, 0, 0, 65553, 0, 0, 98314, 0, 90128,
        0, 0, 0, 65617, 49163, 73824, 90128, 73858, 73729, 90113,
        0, 0, 0, 0, 98434, 73745, 0, 0, 0, 90113,
        0, 90139, 0, 0, 0, 0, 0, 0, 0, 98320,
        73858, 57499, 98305, 0, 98496, 73731, 0, 0, 0, 98432,
        98432, 0, 98432, 73747, 0, 0, 98306, 73738, 90192, 0,
        0, 0, 65749, 90328, 90249, 0, 0, 0, 0, 98305,
        0, 98376, 73818, 57554, 0, 0, 98369, 0, 0, 0,
        0, 98306, 98312, 0, 98370, 73937, 0, 0, 0, 73729,
        90114, 0, 0, 0, 73747, 90129, 0, 0, 90113, 0,
        0, 98368, 0, 0, 0, 0, 0, 90114, 90200, 65554,
        49289, 73744, 0, 0, 73929, 90185, 0, 0,
    ),
)
TAIL_TREES = (
    (
        1588, 0, 63496, 0, 0, 139328, 98369, 0, 61457, 98712,
        0, 131202, 43202, 139272, 0, 90392, 0, 0, 0, 0,
        0, 0, 139329, 0, 131104, 0, 0, 0, 90134, 0,
        139418, 131096, 0, 147585, 0, 0, 147600, 0, 0, 0,
        0, 147611, 0, 0, 0, 0, 0, 139291, 65579, 106713,
        0, 106584, 106688, 0, 0, 147650, 122884, 0, 0, 0,
        0, 147475, 0, 147472, 0, 147480, 131128, 0, 147536, 0,
        0, 0, 131147, 0, 0, 0, 0, 0, 0, 0,
        0, 0, 122914, 0, 0, 0, 0, 0, 0, 0,
        0, 0, 106507, 147472, 0, 147610, 57356, 0, 106587, 0,
        98315, 139392, 147648, 139456, 139338, 0, 0, 0, 0, 0,
        147473, 0, 131080, 0, 147475, 0, 0, 0, 0, 0,
        0, 139409, 0, 0, 90123, 131200, 0, 0,
    ),
    (
        313, 44160, 0, 0, 43012, 0, 102913, 139328, 61572, 0,
        109642, 0, 45568, 0, 0, 0, 98315, 139272, 147584, 139392,
        0, 0, 0, 0, 147464, 0, 147483, 0, 0, 0,
        0, 0, 57767, 98328, 106632, 98328, 0, 139266, 147528, 139336,
        106688, 0, 0, 0, 0, 139411, 0, 139456, 0, 106585,
        147472, 0, 0, 147458, 0, 0, 147466, 0, 0, 0,
        0, 147472, 0, 0, 106626, 147472, 0, 147586, 0, 0,
        0, 0, 131095, 0, 0, 0, 122886, 0, 0, 0,
        0, 106587, 147464, 0, 106506, 147648, 0, 147600, 147466, 0,
        0, 0, 0, 147473, 0, 0, 0, 147458, 0, 0,
        0, 0, 147481, 0, 139281, 0, 0, 0, 98322, 0,
        0, 139674, 131088, 90139, 131081, 0, 0, 131138, 0, 0,
        98307, 0, 0, 139354, 0, 131265, 0, 0,
    ),
    (
        2311, 45584, 62472, 41136, 0, 0, 98498, 139265, 0, 0,
        0, 102417, 0, 90320, 131088, 90626, 98354, 0, 0, 0,
        139267, 0, 139288, 0, 0, 0, 0, 0, 0, 131101,
        0, 0, 57528, 0, 0, 0, 98435, 139328, 0, 139346,
        106499, 147521, 0, 147648, 98883, 139337, 0, 0, 0, 0,
        123049, 0, 0, 0, 0, 0, 0, 0, 0, 0,
        139294, 0, 0, 0, 106512, 123044, 131192, 0, 147587, 0,
        0, 0, 0, 0, 0, 0, 147473, 0, 0, 0,
        65722, 0, 0, 106568, 106689, 147465, 0, 0, 122884, 0,
        0, 0, 106499, 147464, 0, 147602, 0, 98353, 139272, 147465,
        147520, 0, 0, 0, 0, 147475, 0, 0, 0, 139267,
        0, 139280, 0, 0, 0, 90163, 0, 0, 139274, 0,
        0, 0, 0, 139265, 0, 131098, 0, 131106,
    ),
)
SPREAD = 12
TAIL_SPREAD = 18

TREES = len(PANEL_TREES)
TAILS = len(TAIL_TREES)
CHUNKS = 11
PIECE = 64
SPAN = PIECE * CHUNKS
LATE = 9
EXT = 4096
INV = TREES * SPAN
TAIL = -(-2 * NB // (8 * TAILS)) * 8
HELD = INV + TAILS * TAIL
TILE = 512


def swap_lists(pivot_col, pivot_row, row_start, tab_ref):
    lane = lax.broadcasted_iota(I32, (NB, NB), 1)
    sub = lax.broadcasted_iota(I32, (NB, NB), 0)
    low = pivot_col >= NB
    smaller = (pivot_row < pivot_col) & (pivot_row >= NB)
    rank = jnp.sum(jnp.where(smaller, 1.0, 0.0), axis=1, keepdims=True)
    lane_f = lane.astype(F32)
    hit = (rank == lane_f) & low
    landing = jnp.sum(jnp.where(hit, pivot_col.astype(F32), 0.0), axis=0, keepdims=True)
    chosen = jnp.sum(jnp.where(pivot_col == lane, 1.0, 0.0), axis=0, keepdims=True)
    free = jnp.broadcast_to(1.0 - chosen, (NB, NB))
    ahead = jnp.sum(jnp.where(lane < sub, free, 0.0), axis=1, keepdims=True)
    own = jnp.sum(jnp.where(lane == sub, free, 0.0), axis=1, keepdims=True)
    place = (ahead == lane_f) & (own > 0.5)
    displaced = jnp.sum(jnp.where(place, sub.astype(F32), 0.0), axis=0, keepdims=True)
    bound = row_start + lane * TILE
    starts = jnp.sum(jnp.where(low & (pivot_col < bound), 1.0, 0.0), axis=0, keepdims=True)
    tab_ref[...] = jnp.concatenate(
        [landing, displaced, starts, jnp.zeros((5, NB), F32)], axis=0
    ).astype(I32)


def pick(values, bits):
    while len(values) > 1:
        bit, bits = bits[0], bits[1:]
        values = [
            lo if isinstance(lo, int) and isinstance(hi, int) and lo == hi else jnp.where(bit, hi, lo)
            for lo, hi in zip(values[::2], values[1::2])
        ]
    return values[0]


def eliminate(block, packed_ref, linv_ref, binv_ref, upper_ref, scale_ref):
    lane = lax.broadcasted_iota(I32, (8, NB), 1)
    sub = lax.broadcasted_iota(I32, (8, NB), 0)
    groups = NB // 8
    left = tuple(block[8 * q : 8 * q + 8, :] for q in range(groups))
    right = tuple(jnp.where(lane == sub + 8 * q, 1.0, 0.0) for q in range(groups))

    def row_of(x, k):
        return jnp.broadcast_to(x[k : k + 1, :], (8, NB))

    def column_of(x, k):
        return jnp.broadcast_to(x[:, k : k + 1], (8, NB))

    def turn(g, carry):
        a, z = list(carry[0]), list(carry[1])
        active = lane < NB - 8 * g
        upper, linv, scale = a[0], z[0], jnp.zeros((8, NB), F32)
        column = [column_of(a[0], j) for j in range(8)]
        for k in range(8):
            pivot = row_of(column[k], k)
            row_a, row_z = row_of(a[0], k), row_of(z[0], k)
            inverse = 1.0 / pivot
            here = sub == k
            upper = jnp.where(here, row_a, upper)
            linv = jnp.where(here, row_z, linv)
            scale = jnp.where(here, inverse, scale)
            row_a = jnp.where(
                lane > k, jnp.where(active, row_a, 0.0), jnp.where(lane == k, pivot - 1.0, 0.0)
            )
            first = jnp.where(here, 0.0, column[k] * inverse)
            for j in range(k + 1, 8):
                column[j] = column[j] - first * row_of(column[j], k)
            for q in range(groups):
                factor = first if q == 0 else column_of(a[q], k) * inverse
                a[q] = a[q] - factor * row_a
                z[q] = z[q] - factor * row_z
        at = pl.ds(pl.multiple_of(8 * g, 8), 8)
        upper_ref[at, :] = upper
        linv_ref[at, :] = linv
        scale_ref[at, :] = scale
        a = [pltpu.roll(x, NB - 8, 1) for x in a]
        return tuple(a[1:] + a[:1]), tuple(z[1:] + z[:1])

    left, right = lax.fori_loop(0, groups, turn, (left, right))
    for q in range(groups):
        at = slice(8 * q, 8 * q + 8)
        upper = upper_ref[at, :]
        if q:
            upper = pltpu.roll(upper, 8 * q, 1)
        packed_ref[at, :] = jnp.where(lane < sub + 8 * q, left[q], upper)
        binv_ref[at, :] = right[q] * scale_ref[at, :]


def exchange_kernel(
    pivots_sm, pivots_v, matrix, tile_ref, held, incoming_ref, returning_ref, packed_ref, tab_ref,
    rows_ref, other, upper_ref, scale_ref, tab_sm,
    arrive, depart, tail_arrive, tail_depart, swap_sems, local_sems,
):
    plane, chip = lax.axis_index("prow"), lax.axis_index("pcol")
    rows_dev, cols = matrix.shape
    row_start = plane * rows_dev
    root = chip == 0

    @pl.when(root)
    def _():
        for c in range(CHUNKS):
            for t in range(TREES):
                lo = t * SPAN + c * PIECE
                if lo < EXT:
                    pltpu.make_async_copy(
                        matrix.at[pl.ds(lo, PIECE), pl.ds(0, NB)],
                        held.at[pl.ds(lo, PIECE), :],
                        arrive.at[t, c],
                    ).start()
    load = pltpu.make_async_copy(matrix, tile_ref, local_sems.at[0])
    load.start()

    x, y, z = chip % 4, (chip // 4) % 4, chip // 16
    axis_chips = [(x + dx) % 4 + 4 * ((y + dy) % 4) + 16 * ((z + dz) % 8) for dx, dy, dz in HOPS]
    barrier = pltpu.get_barrier_semaphore()
    for there in axis_chips:
        pl.semaphore_signal(barrier, inc=1, device_id=(plane, there), device_id_type=MESH)
    pl.semaphore_signal(barrier, inc=1, device_id=(1 - plane, chip), device_id_type=MESH)

    place = jnp.where(plane == 0, chip, (4 - x) % 4 + 4 * ((4 - y) % 4) + 16 * ((8 - z) % 8))
    bits = [(place // (2**i)) % 2 == 1 for i in range(7)]
    full = 2 ** len(HOPS)
    words = [pick(list(table), bits) for table in PANEL_TREES]
    sends, turns = [w % full for w in words], [w // full for w in words]
    words = [pick(list(table), bits) for table in TAIL_TREES]
    tail_sends, tail_turns = [w % full for w in words], [w // full for w in words]
    mirrored = [HOPS.index(((4 - dx) % 4, (4 - dy) % 4, (8 - dz) % 8)) for dx, dy, dz in HOPS]
    targets = [
        jnp.where(plane == 0, axis_chips[d], axis_chips[mirrored[d]]) for d in range(len(HOPS))
    ]

    pivot_row = jnp.broadcast_to(pivots_v[...], (NB, NB))
    pivot_col = jnp.transpose(pivot_row.astype(F32)).astype(I32)
    swap_lists(pivot_col, pivot_row, row_start, tab_ref)
    move = pltpu.make_async_copy(tab_ref, tab_sm, local_sems.at[1])
    move.start()
    mine = (pivot_col >= row_start) & (pivot_col < row_start + rows_dev)

    pl.semaphore_wait(barrier, len(HOPS) + 1)

    def send(mask, at, out_sems, in_sem):
        for d in range(len(HOPS)):
            @pl.when((mask // (2**d)) % 2 == 1)
            def _():
                pltpu.make_async_remote_copy(
                    src_ref=held.at[at, :], dst_ref=held.at[at, :],
                    send_sem=out_sems.at[d], recv_sem=in_sem,
                    device_id=(plane, targets[d]), device_id_type=MESH,
                ).start()

    def arrived(at, sem):
        pltpu.make_async_copy(held.at[at, :], held.at[at, :], sem).wait()

    def pass_on(s, carry):
        for t in range(TREES):
            c = s - turns[t]
            limit = CHUNKS
            if t == TREES - 1:
                limit = jnp.where(root, LATE, CHUNKS)

            @pl.when((c >= 0) & (c < limit) & (sends[t] > 0))
            def _():
                at = pl.ds(pl.multiple_of(t * SPAN + c * PIECE, 8), PIECE)
                arrived(at, arrive.at[t, c])
                send(sends[t], at, depart.at[t], arrive.at[t, c])
        return carry

    @pl.when(root)
    def _():
        lax.fori_loop(0, CHUNKS, pass_on, 0)

    load.wait()
    move.wait()

    def first(i, carry):
        for j in range(8):
            k = 8 * i + j
            local = jnp.clip(pivots_sm[k] - row_start, 0, rows_dev - 1)
            rows_ref[pl.ds(k, 1), :] = tile_ref[pl.ds(local, 1), :]
        return carry

    lax.fori_loop(0, NB // 8, first, 0)

    def second(i, carry):
        for j in range(8):
            k = 8 * i + j
            local = jnp.clip(tab_sm[1, k], 0, NB - 1)
            rows_ref[pl.ds(NB + k, 1), :] = tile_ref[pl.ds(local, 1), :]
        return carry

    lax.fori_loop(0, FEW // 8, second, 0)

    swaps = []
    for i, part in enumerate((pl.ds(0, NB), pl.ds(NB, cols - NB))):
        swaps.append(pltpu.make_async_remote_copy(
            src_ref=rows_ref.at[:, part], dst_ref=other.at[:, part],
            send_sem=swap_sems.at[i, 0], recv_sem=swap_sems.at[i, 1],
            device_id=(1 - plane, chip), device_id_type=MESH,
        ))
        swaps[i].start()

    @pl.when(chip != 0)
    def _():
        lax.fori_loop(0, SPREAD + CHUNKS, pass_on, 0)

    for i, swap in enumerate(swaps):
        swap.wait()
        for j in range(1 if i == 0 else cols // NB - 1):
            at = slice((i + j) * NB, (i + j + 1) * NB)
            incoming_ref[:, at] = jnp.where(mine, rows_ref[:NB, at], other[:NB, at])
            returning_ref[:, at] = jnp.where(plane == 0, rows_ref[NB:, at], other[NB:, at])
        if i == 0:
            @pl.when(root)
            def _():
                held[EXT : EXT + FEW, :] = returning_ref[:, :NB]
                held[EXT + FEW : INV, :] = jnp.zeros((INV - EXT - FEW, NB), F32)
                t = TREES - 1
                for c in range(LATE, CHUNKS):
                    send(sends[t], pl.ds(t * SPAN + c * PIECE, PIECE), depart.at[t], arrive.at[t, c])
                eliminate(
                    incoming_ref[:, :NB], packed_ref,
                    held.at[INV : INV + NB, :], held.at[INV + NB : INV + 2 * NB, :],
                    upper_ref, scale_ref,
                )
                if HELD > INV + 2 * NB:
                    held[INV + 2 * NB : HELD, :] = jnp.zeros((HELD - INV - 2 * NB, NB), F32)

    def pass_tail(s, carry):
        for t in range(TAILS):
            @pl.when((tail_turns[t] == s) & (tail_sends[t] > 0))
            def _():
                at = pl.ds(INV + t * TAIL, TAIL)

                @pl.when(chip != 0)
                def _():
                    arrived(at, tail_arrive.at[t])
                send(tail_sends[t], at, tail_depart.at[t], tail_arrive.at[t])
        return carry

    lax.fori_loop(0, jnp.where(root, 1, TAIL_SPREAD + 1), pass_tail, 0)

    for t in range(TREES):
        @pl.when((chip != 0) & (sends[t] == 0))
        def _():
            for c in range(CHUNKS):
                arrived(pl.ds(t * SPAN + c * PIECE, PIECE), arrive.at[t, c])
    for t in range(TAILS):
        @pl.when((chip != 0) & (tail_sends[t] == 0))
        def _():
            arrived(pl.ds(INV + t * TAIL, TAIL), tail_arrive.at[t])
    for trees, masks, sems, size in (
        (TREES, sends, depart, SPAN), (TAILS, tail_sends, tail_depart, TAIL)
    ):
        for t in range(trees):
            for d in range(len(HOPS)):
                @pl.when((masks[t] // (2**d)) % 2 == 1)
                def _():
                    arrived(pl.ds(0, size), sems.at[t, d])


def exchange(matrix, pivot_rows):
    rows, cols = matrix.shape
    vmem = pl.BlockSpec(memory_space=pltpu.VMEM)
    return pl.pallas_call(
        exchange_kernel,
        name="exchange",
        out_shape=(
            jax.ShapeDtypeStruct((rows, cols), F32),
            jax.ShapeDtypeStruct((HELD, NB), F32),
            jax.ShapeDtypeStruct((NB, cols), F32),
            jax.ShapeDtypeStruct((FEW, cols), F32),
            jax.ShapeDtypeStruct((NB, NB), F32),
            jax.ShapeDtypeStruct((8, NB), I32),
        ),
        in_specs=[
            pl.BlockSpec(memory_space=pltpu.SMEM), vmem, pl.BlockSpec(memory_space=pltpu.HBM),
        ],
        out_specs=(vmem,) * 6,
        scratch_shapes=[
            pltpu.VMEM((NB + FEW, cols), F32),
            pltpu.VMEM((NB + FEW, cols), F32),
            pltpu.VMEM((NB, NB), F32),
            pltpu.VMEM((NB, NB), F32),
            pltpu.SMEM((8, NB), I32),
            pltpu.SemaphoreType.DMA((TREES, CHUNKS)),
            pltpu.SemaphoreType.DMA((TREES, len(HOPS))),
            pltpu.SemaphoreType.DMA((TAILS,)),
            pltpu.SemaphoreType.DMA((TAILS, len(HOPS))),
            pltpu.SemaphoreType.DMA((2, 2)),
            pltpu.SemaphoreType.DMA((2,)),
        ],
        compiler_params=pltpu.CompilerParams(
            collective_id=0, has_side_effects=True, vmem_limit_bytes=44 * 2**20
        ),
    )(pivot_rows, pivot_rows.reshape(1, NB), matrix)


SLOTS = 3


def update_kernel(
    tab, tile_ref, held, incoming_ref, returning_ref, packed_ref, out_ref,
    slots, right, patch, sems,
):
    plane, first = lax.axis_index("prow"), lax.axis_index("pcol") == 0
    rows = tile_ref.shape[0]

    def product(left_f32):
        high = left_f32.astype(BF16)
        low = (left_f32 - high.astype(F32)).astype(BF16)
        return jnp.dot(
            jnp.concatenate([high, high, low], axis=1), right[...], preferred_element_type=F32
        )

    def keep(block):
        return jnp.concatenate([jnp.where(first, 0.0, block[:, :NB]), block[:, NB:]], axis=1)

    source = incoming_ref[...]
    lane = lax.broadcasted_iota(I32, (NB, NB), 1)
    sub = lax.broadcasted_iota(I32, (NB, NB), 0)
    packed = packed_ref[...]
    unit = jnp.where(lane < sub, packed, jnp.where(lane == sub, 1.0, 0.0))
    w = jnp.dot(
        held[INV + NB : INV + 2 * NB, :],
        jnp.concatenate([jnp.where(first, -unit, source[:, :NB]), source[:, NB:]], axis=1),
        precision=HIGH, preferred_element_type=F32,
    )
    high = w.astype(BF16)
    right[0:NB, :] = high
    right[NB : 2 * NB, :] = (w - high.astype(F32)).astype(BF16)
    right[2 * NB :, :] = high
    patch[...] = keep(returning_ref[...]) - product(held[EXT : EXT + FEW, :])

    copies = []
    for j in range(rows // TILE):
        slot = slots.at[j % SLOTS]
        if j >= SLOTS:
            copies[j - SLOTS].wait()
        at = slice(j * TILE, (j + 1) * TILE)
        slot[...] = keep(tile_ref[at, :]) - product(held[at, :])
        if j == 0:
            @pl.when(plane == 0)
            def _():
                upper = jnp.dot(
                    held[INV : INV + NB, :], source, precision=HIGH, preferred_element_type=F32
                )
                slot[0:NB, :] = jnp.concatenate(
                    [jnp.where(first, packed, upper[:, :NB]), upper[:, NB:]], axis=1
                )
        base = plane * rows + j * TILE

        def land(i, carry):
            slot[pl.ds(tab[0, i] - base, 1), :] = patch[pl.ds(i, 1), :]
            return carry

        lax.fori_loop(tab[2, j], tab[2, j + 1], land, 0)
        copies.append(pltpu.make_async_copy(slot, out_ref.at[at, :], sems.at[j % SLOTS]))
        copies[j].start()
    for copy in copies[-SLOTS:]:
        copy.wait()


def update(tile, held, incoming, returning, packed, tab):
    rows, cols = tile.shape
    vmem = pl.BlockSpec(memory_space=pltpu.VMEM)
    return pl.pallas_call(
        update_kernel,
        name="update",
        out_shape=jax.ShapeDtypeStruct((rows, cols), F32),
        in_specs=[pl.BlockSpec(memory_space=pltpu.SMEM)] + [vmem] * 5,
        out_specs=pl.BlockSpec(memory_space=pltpu.HBM),
        scratch_shapes=[
            pltpu.VMEM((SLOTS, TILE, cols), F32),
            pltpu.VMEM((3 * NB, cols), BF16),
            pltpu.VMEM((FEW, cols), F32),
            pltpu.SemaphoreType.DMA((SLOTS,)),
        ],
        compiler_params=pltpu.CompilerParams(vmem_limit_bytes=24 * 2**20),
    )(tab, tile, held, incoming, returning, packed)


def on_device(matrix, pivot_rows):
    tile, held, incoming, returning, packed, tab = exchange(matrix, pivot_rows)
    return update(tile, held, incoming, returning, packed, tab)


def solution(mesh):
    return jax.shard_map(
        on_device, mesh=mesh, in_specs=(P("prow", "pcol"), P()), out_specs=P("prow", "pcol"), check_vma=False
    )
```

```python
import functools

import jax
import jax.numpy as jnp
from jax import lax
from jax.experimental import pallas as pl
from jax.experimental.pallas import tpu as pltpu
from jax.sharding import PartitionSpec as P

NB = 128
FEW = 96
F32 = jnp.float32
BF16 = jnp.bfloat16
I32 = jnp.int32
HIGH = lax.Precision.HIGHEST
MESH = pl.DeviceIdType.MESH

HOPS = (
    (1, 0, 0), (3, 0, 0), (2, 0, 0), (0, 1, 0), (0, 3, 0), (0, 2, 0),
    (0, 0, 1), (0, 0, 7), (0, 0, 2), (0, 0, 6), (0, 0, 3), (0, 0, 5), (0, 0, 4),
)
FAN = 4
PANEL_TREES = (
    (
        0, 0, 1537, 0, 6367233, 18480, 2060, 14352, 234930336, 624,
        112, 515, 0, 4, 0, 14337, 0, 0, 0, 0,
        12, 196996, 1540, 2052, 4, 515, 0, 4, 0, 0,
        0, 3, 0, 0, 0, 112, 0, 196993, 12, 12,
        513, 1, 513, 0, 3, 0, 0, 16, 112, 1539,
        0, 0, 4, 235078145, 1537, 12, 3, 2049, 4, 0,
        0, 14339, 0, 0, 196993, 12, 0, 0, 79884, 0,
        3, 4, 16, 0, 0, 515, 0, 0, 0, 0,
        0, 0, 112, 262284, 18612609, 25428481, 1837068, 235144708, 0, 262657,
        16, 16, 2050, 0, 14352, 16, 0, 0, 0, 0,
        12, 12, 12, 1, 0, 0, 0, 1, 0, 0,
        0, 0, 0, 0, 12, 0, 12, 12, 1539, 196739,
        515, 4, 0, 0, 0, 112, 0, 0,
    ),
    (
        0, 0, 0, 0, 0, 4, 131, 0, 12, 0,
        12, 0, 34091010, 0, 235089952, 0, 1, 1, 0, 0,
        3, 0, 0, 0, 0, 0, 1539, 14337, 132, 112,
        0, 234946956, 388, 16, 262659, 0, 63489, 112, 0, 0,
        400, 0, 63504, 0, 2294275, 0, 34080260, 112, 0, 0,
        0, 0, 3, 0, 0, 0, 197121, 1540, 12, 0,
        4, 0, 1, 0, 0, 3, 0, 14352, 385, 0,
        0, 0, 263683, 0, 0, 112, 196993, 263684, 197128, 4,
        0, 0, 515, 0, 385, 0, 0, 0, 0, 0,
        385, 0, 4, 0, 17924, 0, 515, 0, 3, 515,
        1837057, 2049, 0, 16, 400, 4, 2051, 0, 235078240, 0,
        30732, 0, 0, 16, 2049, 16, 12, 0, 0, 0,
        528, 0, 1537, 0, 0, 1540, 16899, 0,
    ),
    (
        0, 4, 0, 0, 3, 0, 0, 1648, 0, 0,
        0, 0, 63584, 0, 4, 0, 6488608, 0, 3, 12,
        240, 1, 14352, 0, 3, 1, 16, 12, 1537, 235144705,
        14340, 16, 0, 1, 0, 1, 0, 0, 0, 1,
        0, 12, 0, 0, 0, 17924, 0, 2060, 17411, 197121,
        16, 14340, 0, 528, 0, 63520, 235079683, 0, 16, 3,
        112, 144, 0, 0, 0, 0, 1, 0, 0, 513,
        0, 0, 1539, 0, 0, 12, 112, 4, 0, 3,
        112, 1, 0, 0, 0, 0, 0, 385, 0, 12,
        0, 1, 79875, 197121, 12, 624, 0, 1, 4, 0,
        0, 0, 0, 1, 0, 196993, 0, 1837068, 10224001, 30724,
        0, 67596, 1, 144, 0, 0, 0, 0, 0, 1,
        2049, 263792, 2060, 16, 197121, 1, 12, 4,
    ),
    (
        0, 3933700, 0, 79904, 4, 14416, 0, 132, 0, 0,
        3, 624, 0, 14337, 1552, 0, 0, 3, 0, 4,
        0, 0, 14339, 131, 0, 0, 0, 385, 0, 12,
        8651137, 1, 1537, 262768, 0, 235143681, 0, 0, 0, 18436,
        0, 0, 0, 240, 1, 2060, 12, 0, 12, 0,
        1836548, 33751425, 0, 0, 14339, 2052, 0, 0, 0, 2049,
        16, 0, 2060, 14352, 0, 1, 0, 0, 14348, 1539,
        0, 3, 0, 1835523, 0, 0, 0, 0, 0, 16,
        0, 0, 1, 0, 1540, 234946945, 2360836, 0, 16, 276484,
        235143681, 0, 0, 515, 0, 0, 12, 515, 0, 12,
        0, 3, 1, 0, 0, 0, 0, 0, 0, 0,
        262659, 1539, 524, 14339, 4, 14339, 0, 0, 4, 0,
        0, 0, 3, 1540, 2060, 0, 0, 0,
    ),
    (
        0, 0, 0, 0, 0, 1539, 0, 0, 0, 3,
        2052, 0, 0, 12, 0, 0, 0, 0, 112, 0,
        1, 16, 0, 14348, 0, 0, 0, 0, 14339, 4,
        0, 14348, 112, 396, 112, 0, 624, 0, 112, 79875,
        112, 14337, 0, 0, 112, 14337, 14337, 0, 25231745, 1837057,
        112, 14352, 1835393, 1, 16, 2160, 0, 8128513, 513, 0,
        14337, 12, 0, 0, 0, 2060, 16, 1539, 0, 0,
        16, 2049, 0, 263683, 0, 2051, 0, 2049, 16, 235143308,
        112, 515, 1, 0, 0, 0, 0, 0, 12, 0,
        0, 0, 0, 3, 0, 0, 49284, 196740, 0, 0,
        388, 513, 0, 0, 14340, 0, 14340, 4, 16, 0,
        0, 0, 1835139, 65676, 1540, 262664, 4, 2051, 16, 0,
        0, 0, 63504, 33634307, 0, 16, 0, 0,
    ),
    (
        0, 0, 79904, 235929992, 0, 12, 131, 0, 12, 4,
        3, 2158608, 0, 1, 0, 0, 0, 515, 1, 0,
        0, 0, 0, 0, 33751172, 0, 12, 49312, 112, 0,
        385, 0, 0, 112, 235078147, 0, 0, 2051, 33620353, 112,
        0, 0, 385, 0, 0, 2051, 1835393, 4, 112, 0,
        0, 0, 0, 0, 1, 0, 2049, 0, 0, 513,
        0, 0, 0, 513, 210960, 14340, 235078024, 65667, 14352, 0,
        0, 1, 0, 0, 235144707, 0, 0, 0, 235143553, 0,
        2051, 12, 515, 0, 0, 0, 385, 0, 0, 0,
        0, 14340, 0, 0, 0, 1, 0, 0, 3, 12,
        0, 0, 0, 12, 235078145, 235144708, 263684, 8128001, 0, 0,
        0, 0, 0, 3, 10224096, 1540, 1, 0, 0, 1,
        0, 0, 0, 1, 0, 0, 3, 33572355,
    ),
)
TAIL_TREES = (
    (
        0, 0, 2363404, 0, 1837104, 0, 0, 0, 1839106, 0,
        25223264, 0, 0, 0, 6322224, 0, 0, 112, 196993, 1,
        16899, 0, 0, 112, 513, 0, 0, 0, 0, 0,
        33751425, 0, 0, 0, 6308384, 0, 12, 0, 112, 0,
        8437920, 33751553, 0, 235144708, 16, 0, 0, 0, 0, 0,
        0, 0, 27001217, 1537, 0, 2060, 0, 0, 0, 0,
        0, 0, 25231745, 0, 0, 0, 515, 12, 1537, 0,
        0, 0, 1835393, 0, 0, 0, 1, 0, 0, 0,
        33620364, 0, 0, 235144708, 1835521, 263684, 0, 515, 16, 0,
        0, 0, 1837058, 0, 235078147, 16, 513, 1, 0, 2052,
        0, 0, 0, 0, 0, 0, 197121, 0, 1, 0,
        0, 0, 0, 0, 0, 0, 1, 263681, 0, 0,
        65921, 14340, 0, 2060, 2052, 0, 197121, 0,
    ),
    (
        0, 0, 0, 206896, 1839105, 25231536, 12, 0, 0, 0,
        0, 12, 0, 0, 0, 1836576, 25231490, 12, 1544, 0,
        3, 0, 0, 263684, 112, 0, 235144707, 0, 14348, 1837088,
        112, 0, 0, 0, 0, 1, 513, 235078145, 0, 0,
        0, 0, 0, 0, 0, 0, 0, 235078017, 0, 0,
        235078147, 235143560, 0, 2052, 0, 0, 0, 0, 0, 25231745,
        0, 0, 0, 0, 234948097, 263688, 0, 1539, 14340, 0,
        0, 0, 0, 0, 0, 0, 14338, 0, 0, 0,
        0, 0, 0, 6308360, 0, 0, 0, 14339, 197121, 0,
        0, 1835523, 0, 0, 0, 0, 3670280, 263684, 33751172, 2060,
        0, 14352, 33583106, 0, 1837058, 0, 33603808, 0, 0, 1837059,
        112, 0, 0, 0, 0, 0, 1539, 0, 0, 4,
        513, 0, 0, 0, 0, 0, 0, 3,
    ),
    (
        0, 1544, 0, 235149316, 0, 3, 4, 234946976, 0, 235144752,
        0, 1, 4098, 112, 2144, 0, 0, 0, 1835523, 197123,
        0, 0, 0, 1, 0, 196993, 0, 0, 0, 0,
        0, 1537, 14340, 0, 0, 0, 0, 0, 0, 25231746,
        0, 0, 0, 0, 25231490, 1836548, 197121, 0, 0, 0,
        0, 17924, 0, 0, 0, 385, 0, 25231745, 0, 0,
        0, 0, 0, 33751425, 0, 1836547, 1835144, 0, 0, 0,
        0, 0, 4, 0, 0, 0, 0, 0, 0, 0,
        8406018, 276492, 197232, 0, 235143553, 112, 14352, 1837068, 235143553, 1837057,
        0, 14352, 0, 2051, 14337, 0, 0, 0, 0, 1,
        1, 0, 0, 0, 4, 0, 0, 0, 0, 0,
        197121, 0, 1, 0, 0, 8128001, 0, 0, 0, 385,
        0, 196993, 0, 0, 0, 1, 0, 263681,
    ),
)
TURNS = (
    (
        0, 111616, 11, 98304, 270339, 11698629, 360, 175109, 453, 13631496,
        15040811, 262152, 3168, 11698187, 275648, 11, 3328, 459104, 15741952, 300032,
        12588491, 15736840, 470027, 16089096, 8205, 11275, 13792, 470475, 12588192, 16163072,
        371712, 16163181, 12878112, 9811424, 12583296, 207885, 9437536, 460, 15728655, 12892171,
        12583209, 15741963, 398, 360448, 9797835, 13052928, 16154912, 11566, 4560911, 7349260,
        9808896, 7644160, 7340492, 9448457, 13041676, 9808911, 9583, 12583372, 15744495, 471040,
        7813568, 9448463, 459136, 360448, 12, 9929199, 12597248, 9437664, 492009, 407552,
        15728655, 13041676, 12684, 16220160, 0, 15744495, 11552, 12597632, 15729056, 13056384,
        15739904, 12597248, 16220655, 12, 393671, 294921, 393228, 15369, 14123008, 407564,
        492015, 14348, 9514, 16231424, 14733, 11279, 5603616, 8662016, 14784, 262496,
        8388975, 11895244, 491535, 14796, 11534624, 13792, 14680448, 11545615, 13637824, 9216,
        426272, 369664, 3416064, 5418432, 8651117, 5407168, 11534795, 8388621, 11894795, 13320,
        8552, 11275, 11974112, 9811968, 365568, 8397165, 11552, 11264,
    ),
    (
        0, 458752, 453, 473091, 14784, 671755, 642056, 524288, 457, 557067,
        585, 642054, 458752, 524302, 557600, 16384, 14336, 17038, 640555, 524928,
        16896, 0, 0, 642656, 20075, 655360, 20491, 9, 16398, 19456,
        21134, 622592, 655360, 11, 585, 20480, 18048, 20494, 651, 655374,
        576, 640, 14, 640, 557696, 655374, 655371, 20494, 13, 0,
        20480, 608256, 576, 21120, 14, 656000, 15, 688128, 0, 21516,
        0, 0, 672, 655375, 18442, 675853, 688810, 21127, 21133, 0,
        0, 10, 688800, 0, 13, 0, 21120, 0, 13, 0,
        492013, 589838, 589835, 19008, 590400, 656000, 688142, 676480, 610944, 688128,
        0, 709644, 576, 655360, 688800, 655, 14912, 18048, 18443, 643727,
        655360, 20480, 20480, 12, 706572, 15, 22188, 9, 640, 20480,
        675840, 0, 622592, 11, 8, 524293, 16907, 608, 0, 642056,
        21024, 656000, 0, 651, 640, 622592, 651, 642056,
    ),
)
PANEL_ROOT = ((4,), (12,), (16, 12), (1, 3), (48, 112), (3,))
TAIL_ROOT = ((2, 8, 80, 4), (96, 3, 4, 16), (80, 1, 3, 12))
SPREAD = 15
TAIL_SPREAD = 21

TREES = len(PANEL_TREES)
TAILS = len(TAIL_TREES)
PIECE = 64
PANEL = 4096
CHUNKS = tuple(PANEL // PIECE // TREES + (t < PANEL // PIECE % TREES) for t in range(TREES))
MOST = CHUNKS[0]
FIRST = tuple(sum(CHUNKS[:t]) * PIECE for t in range(TREES))
INV = PANEL
TAIL = -(-2 * NB // (8 * TAILS)) * 8
HELD = INV + TAILS * TAIL
SOON = 2
EARLY = 4
TILE = 512


def swap_lists(pivot_col, pivot_row, row_start, tab_ref):
    lane = lax.broadcasted_iota(I32, (NB, NB), 1)
    sub = lax.broadcasted_iota(I32, (NB, NB), 0)
    low = pivot_col >= NB
    smaller = (pivot_row < pivot_col) & (pivot_row >= NB)
    rank = jnp.sum(jnp.where(smaller, 1.0, 0.0), axis=1, keepdims=True)
    lane_f = lane.astype(F32)
    hit = (rank == lane_f) & low
    landing = jnp.sum(jnp.where(hit, pivot_col.astype(F32), 0.0), axis=0, keepdims=True)
    chosen = jnp.sum(jnp.where(pivot_col == lane, 1.0, 0.0), axis=0, keepdims=True)
    free = jnp.broadcast_to(1.0 - chosen, (NB, NB))
    ahead = jnp.sum(jnp.where(lane < sub, free, 0.0), axis=1, keepdims=True)
    own = jnp.sum(jnp.where(lane == sub, free, 0.0), axis=1, keepdims=True)
    place = (ahead == lane_f) & (own > 0.5)
    displaced = jnp.sum(jnp.where(place, sub.astype(F32), 0.0), axis=0, keepdims=True)
    bound = row_start + lane * TILE
    starts = jnp.sum(jnp.where(low & (pivot_col < bound), 1.0, 0.0), axis=0, keepdims=True)
    tab_ref[...] = jnp.concatenate(
        [landing, displaced, starts, jnp.zeros((5, NB), F32)], axis=0
    ).astype(I32)


def pick(values, bits):
    while len(values) > 1:
        bit, bits = bits[0], bits[1:]
        values = [
            lo if isinstance(lo, int) and isinstance(hi, int) and lo == hi else jnp.where(bit, hi, lo)
            for lo, hi in zip(values[::2], values[1::2])
        ]
    return values[0]


def eliminate(
    block, packed_ref, linv_ref, binv_ref, upper_ref, scale_ref, busy_turns, busy, between
):
    lane = lax.broadcasted_iota(I32, (8, NB), 1)
    sub = lax.broadcasted_iota(I32, (8, NB), 0)
    groups = NB // 8
    rows = tuple(block[8 * q : 8 * q + 8, :] for q in range(groups))
    lower = tuple(jnp.zeros((8, NB), F32) for q in range(groups))

    def row_of(x, k):
        return jnp.broadcast_to(x[k : k + 1, :], (8, NB))

    def column_of(x, k):
        return jnp.broadcast_to(x[:, k : k + 1], (8, NB))

    def turn(g, carry, also=None):
        if also is not None:
            also(g)
        a, low = list(carry[0]), list(carry[1])
        seen, scale = a[0], jnp.zeros((8, NB), F32)
        column = [column_of(a[0], j) for j in range(8)]
        for k in range(8):
            pivot = row_of(column[k], k)
            row = row_of(a[0], k)
            inverse = 1.0 / pivot
            here = sub == k
            seen = jnp.where(here, row, seen)
            scale = jnp.where(here, inverse, scale)
            row = jnp.where(lane == k, pivot + 1.0, row)
            first = jnp.where(here, 0.0, column[k] * inverse)
            for j in range(k + 1, 8):
                column[j] = column[j] - first * row_of(column[j], k)
            kept = lane == 8 * g + k
            for q in range(groups):
                factor = first if q == 0 else column_of(a[q], k) * inverse
                a[q] = a[q] - factor * row
                low[q] = jnp.where(kept, factor, low[q])
            a[0] = jnp.where(here & (lane == k), 1.0, a[0])
        at = pl.ds(pl.multiple_of(8 * g, 8), 8)
        upper_ref[at, :] = seen
        scale_ref[at, :] = scale
        a = [pltpu.roll(x, NB - 8, 1) for x in a]
        return tuple(a[1:] + a[:1]), tuple(low[1:] + low[:1])

    carry = lax.fori_loop(0, busy_turns, functools.partial(turn, also=busy), (rows, lower))
    between()
    rows, lower = lax.fori_loop(busy_turns, groups, turn, carry)
    for q in range(groups):
        at = slice(8 * q, 8 * q + 8)
        seen = upper_ref[at, :]
        if q:
            seen = pltpu.roll(seen, 8 * q, 1)
        below = lane < sub + 8 * q
        packed_ref[at, :] = jnp.where(below, lower[q], seen)
        linv_ref[at, :] = jnp.where(below, seen, jnp.where(lane == sub + 8 * q, 1.0, 0.0))
        binv_ref[at, :] = rows[q] * scale_ref[at, :]


def exchange_kernel(
    pivots, matrix, tile_ref, held, incoming_ref, returning_ref, packed_ref, tab_ref,
    rows_ref, other, linv_ref, upper_ref, scale_ref, pivots_v, pivots_sm, tab_sm,
    arrive, depart, tail_arrive, tail_depart, root_depart, swap_sems, local_sems,
):
    plane, chip = lax.axis_index("prow"), lax.axis_index("pcol")
    rows_dev, cols = matrix.shape
    row_start = plane * rows_dev
    root = chip == 0

    fetch_sm = pltpu.make_async_copy(pivots, pivots_sm, local_sems.at[2])
    fetch_v = pltpu.make_async_copy(pivots, pivots_v, local_sems.at[3])
    fetch_v.start()
    fetch_sm.start()

    @pl.when(root)
    def _():
        for c in range(MOST):
            for t in range(TREES):
                if c < CHUNKS[t]:
                    lo = FIRST[t] + c * PIECE
                    pltpu.make_async_copy(
                        matrix.at[pl.ds(lo, PIECE), pl.ds(0, NB)],
                        held.at[pl.ds(lo, PIECE), :],
                        arrive.at[t, c],
                    ).start()
    load = pltpu.make_async_copy(matrix, tile_ref, local_sems.at[0])
    load.start()

    x, y, z = chip % 4, (chip // 4) % 4, chip // 16
    barrier = pltpu.get_barrier_semaphore()
    for dx, dy, dz in HOPS:
        there = (x + dx) % 4 + 4 * ((y + dy) % 4) + 16 * ((z + dz) % 8)
        pl.semaphore_signal(barrier, inc=1, device_id=(plane, there), device_id_type=MESH)
    pl.semaphore_signal(barrier, inc=1, device_id=(1 - plane, chip), device_id_type=MESH)

    fetch_v.wait()
    pivot_row = jnp.broadcast_to(pivots_v[...], (NB, NB))
    pivot_col = jnp.transpose(pivot_row.astype(F32)).astype(I32)
    swap_lists(pivot_col, pivot_row, row_start, tab_ref)
    move = pltpu.make_async_copy(tab_ref, tab_sm, local_sems.at[1])
    move.start()
    mine = (pivot_col >= row_start) & (pivot_col < row_start + rows_dev)

    def gather_pivots():
        fetch_sm.wait()
        load.wait()

        def some(i, carry):
            for j in range(8):
                k = 8 * i + j
                local = jnp.clip(pivots_sm[0, k] - row_start, 0, rows_dev - 1)
                rows_ref[pl.ds(k, 1), :] = tile_ref[pl.ds(local, 1), :]
            return carry

        lax.fori_loop(0, NB // 8, some, 0)
        swaps[0].start()
        swaps[1].start()

    def swap_of(i, rows, columns):
        return pltpu.make_async_remote_copy(
            src_ref=rows_ref.at[rows, columns], dst_ref=other.at[rows, columns],
            send_sem=swap_sems.at[i, 0], recv_sem=swap_sems.at[i, 1],
            device_id=(1 - plane, chip), device_id_type=MESH,
        )

    swaps = [
        swap_of(0, pl.ds(0, NB), pl.ds(0, NB)),
        swap_of(1, pl.ds(0, NB), pl.ds(NB, cols - NB)),
        swap_of(2, pl.ds(NB, FEW), pl.ds(0, cols)),
    ]

    def gather_displaced():
        move.wait()

        def some(i, carry):
            for j in range(8):
                k = 8 * i + j
                local = jnp.clip(tab_sm[1, k], 0, NB - 1)
                rows_ref[pl.ds(NB + k, 1), :] = tile_ref[pl.ds(local, 1), :]
            return carry

        lax.fori_loop(0, FEW // 8, some, 0)
        swaps[2].start()

    def merge(at):
        incoming_ref[:, at] = jnp.where(mine, rows_ref[:NB, at], other[:NB, at])

    def merge_rest():
        for j in range(1, cols // NB):
            merge(slice(j * NB, (j + 1) * NB))
        returning_ref[...] = jnp.where(plane == 0, rows_ref[NB:, :], other[NB:, :])

    def arrived(at, sem):
        pltpu.make_async_copy(held.at[at, :], held.at[at, :], sem).wait()

    def send(at, out_sem, in_sem, there):
        pltpu.make_async_remote_copy(
            src_ref=held.at[at, :], dst_ref=held.at[at, :], send_sem=out_sem, recv_sem=in_sem,
            device_id=(plane, there), device_id_type=MESH,
        ).start()

    def piece(t, c):
        return pl.ds(pl.multiple_of(FIRST[t] + c * PIECE, 8), PIECE)

    def tail(t):
        return pl.ds(INV + t * TAIL, TAIL)

    def offset(code):
        dx, dy, dz = code % 4, (code // 4) % 4, code // 16
        mirror = (4 - dx) % 4 + 4 * ((4 - dy) % 4) + 16 * ((8 - dz) % 8)
        return jnp.where(plane == 0, code, mirror)

    def steps(word):
        return [(word // 128**i) % 128 for i in range(FAN)]

    @pl.when(root)
    def _():
        def spread(c, trees=range(TREES)):
            for t in trees:
                at = piece(t, c)
                for i, code in enumerate(PANEL_ROOT[t]):
                    send(at, root_depart.at[t, i], arrive.at[t, c], offset(code))

        def staged(c):
            for t in range(TREES):
                if c < CHUNKS[t]:
                    arrived(piece(t, c), arrive.at[t, c])

        pl.semaphore_wait(barrier, len(HOPS) + 1)
        for c in range(SOON):
            staged(c)
            spread(c)
        gather_pivots()
        gather_displaced()
        for c in range(SOON, MOST):
            staged(c)
        for c in range(SOON, EARLY):
            spread(c)
        swaps[0].wait()
        merge(slice(0, NB))
        eliminate(
            incoming_ref[:, :NB], packed_ref, linv_ref, held.at[INV + NB : INV + 2 * NB, :],
            upper_ref, scale_ref, CHUNKS[-1] - EARLY, lambda g: spread(g + EARLY),
            lambda: spread(MOST - 1, [t for t in range(TREES) if CHUNKS[t] == MOST]),
        )
        swaps[1].wait()
        swaps[2].wait()
        held[INV : INV + NB, :] = linv_ref[...]

        @pl.when(plane == 1)
        def _():
            held[INV : INV + FEW, :] = other[NB:, :NB]

        if HELD > INV + 2 * NB:
            held[INV + 2 * NB : HELD, :] = jnp.zeros((HELD - INV - 2 * NB, NB), F32)
        for t in range(TAILS):
            for i, code in enumerate(TAIL_ROOT[t]):
                send(tail(t), root_depart.at[TREES + t, i], tail_arrive.at[t], offset(code))
        merge_rest()
        for t in range(TREES + TAILS):
            for i in range(len((PANEL_ROOT + TAIL_ROOT)[t])):
                at = pl.ds(0, CHUNKS[t] * PIECE if t < TREES else TAIL)
                arrived(at, root_depart.at[t, i])

    @pl.when(chip != 0)
    def _():
        place = jnp.where(plane == 0, chip, (4 - x) % 4 + 4 * ((4 - y) % 4) + 16 * ((8 - z) % 8))
        bits = [(place // (2**i)) % 2 == 1 for i in range(7)]

        def chips_of(word):
            codes, there = steps(word), []
            for code in codes:
                dx, dy, dz = code % 4, (code // 4) % 4, code // 16
                sign = 1 - 2 * plane
                there.append(
                    (x + sign * dx + 4) % 4 + 4 * ((y + sign * dy + 4) % 4)
                    + 16 * ((z + sign * dz + 8) % 8)
                )
            return codes, there

        panel = [chips_of(pick(list(table), bits)) for table in PANEL_TREES]
        turn_words = [pick(list(table), bits) for table in TURNS]
        turns = [(turn_words[t // 5] // 32 ** (t % 5)) % 32 for t in range(TREES + TAILS)]
        tails = [chips_of(pick(list(table), bits)) for table in TAIL_TREES]
        pl.semaphore_wait(barrier, len(HOPS) + 1)
        gather_pivots()
        gather_displaced()

        def send_all(node, at, out_sems, in_sem):
            codes, there = node
            send(at, out_sems.at[0], in_sem, there[0])

            @pl.when(codes[1] > 0)
            def _():
                send(at, out_sems.at[1], in_sem, there[1])

                @pl.when(codes[2] > 0)
                def _():
                    send(at, out_sems.at[2], in_sem, there[2])

                    @pl.when(codes[3] > 0)
                    def _():
                        send(at, out_sems.at[3], in_sem, there[3])

        def pass_on(s, carry):
            for t in range(TREES):
                c = s - turns[t]

                @pl.when((c >= 0) & (c < CHUNKS[t]) & (panel[t][0][0] > 0))
                def _():
                    at = piece(t, c)
                    arrived(at, arrive.at[t, c])
                    send_all(panel[t], at, depart.at[t], arrive.at[t, c])
            for t in range(TAILS):
                @pl.when((turns[TREES + t] == s) & (tails[t][0][0] > 0))
                def _():
                    arrived(tail(t), tail_arrive.at[t])
                    send_all(tails[t], tail(t), tail_depart.at[t], tail_arrive.at[t])
            return carry

        lax.fori_loop(1, max(SPREAD + MOST, TAIL_SPREAD + 1), pass_on, 0)
        for swap in swaps:
            swap.wait()
        merge(slice(0, NB))
        merge_rest()

        for t in range(TREES):
            @pl.when(panel[t][0][0] == 0)
            def _():
                for c in range(CHUNKS[t]):
                    arrived(piece(t, c), arrive.at[t, c])
        for t in range(TAILS):
            @pl.when(tails[t][0][0] == 0)
            def _():
                arrived(tail(t), tail_arrive.at[t])
        for t in range(TREES + TAILS):
            codes = (panel + tails)[t][0]
            for i in range(FAN):
                @pl.when(codes[i] > 0)
                def _():
                    if t < TREES:
                        arrived(pl.ds(0, CHUNKS[t] * PIECE), depart.at[t, i])
                    else:
                        arrived(pl.ds(0, TAIL), tail_depart.at[t - TREES, i])


def exchange(matrix, pivot_rows):
    rows, cols = matrix.shape
    vmem = pl.BlockSpec(memory_space=pltpu.VMEM)
    return pl.pallas_call(
        exchange_kernel,
        name="exchange",
        out_shape=(
            jax.ShapeDtypeStruct((rows, cols), F32),
            jax.ShapeDtypeStruct((HELD, NB), F32),
            jax.ShapeDtypeStruct((NB, cols), F32),
            jax.ShapeDtypeStruct((FEW, cols), F32),
            jax.ShapeDtypeStruct((NB, NB), F32),
            jax.ShapeDtypeStruct((8, NB), I32),
        ),
        in_specs=[pl.BlockSpec(memory_space=pltpu.HBM)] * 2,
        out_specs=(vmem,) * 6,
        scratch_shapes=[
            pltpu.VMEM((NB + FEW, cols), F32),
            pltpu.VMEM((NB + FEW, cols), F32),
            pltpu.VMEM((NB, NB), F32),
            pltpu.VMEM((NB, NB), F32),
            pltpu.VMEM((NB, NB), F32),
            pltpu.VMEM((1, NB), I32),
            pltpu.SMEM((1, NB), I32),
            pltpu.SMEM((8, NB), I32),
            pltpu.SemaphoreType.DMA((TREES, MOST)),
            pltpu.SemaphoreType.DMA((TREES, FAN)),
            pltpu.SemaphoreType.DMA((TAILS,)),
            pltpu.SemaphoreType.DMA((TAILS, FAN)),
            pltpu.SemaphoreType.DMA((TREES + TAILS, max(map(len, PANEL_ROOT + TAIL_ROOT)))),
            pltpu.SemaphoreType.DMA((3, 2)),
            pltpu.SemaphoreType.DMA((4,)),
        ],
        compiler_params=pltpu.CompilerParams(
            collective_id=0, has_side_effects=True, vmem_limit_bytes=44 * 2**20
        ),
    )(pivot_rows.reshape(1, NB), matrix)


SLOTS = 3


def update_kernel(
    tab, tile_ref, held, incoming_ref, returning_ref, packed_ref, out_ref,
    slots, right, patch, ext, sems,
):
    plane, first = lax.axis_index("prow"), lax.axis_index("pcol") == 0
    rows = tile_ref.shape[0]

    def product(left_f32):
        high = left_f32.astype(BF16)
        low = (left_f32 - high.astype(F32)).astype(BF16)
        return jnp.dot(
            jnp.concatenate([high, high, low], axis=1), right[...], preferred_element_type=F32
        )

    def keep(block):
        return jnp.concatenate([jnp.where(first, 0.0, block[:, :NB]), block[:, NB:]], axis=1)

    @pl.when(plane == 1)
    def _():
        ext[...] = held[INV : INV + FEW, :]

    @pl.when(plane == 0)
    def _():
        def take(i, carry):
            for k in range(8):
                row = jnp.clip(tab[1, 8 * i + k], 0, NB - 1)
                ext[pl.ds(8 * i + k, 1), :] = held[pl.ds(row, 1), :]
            return carry

        lax.fori_loop(0, FEW // 8, take, 0)

    source = incoming_ref[...]
    lane = lax.broadcasted_iota(I32, (NB, NB), 1)
    sub = lax.broadcasted_iota(I32, (NB, NB), 0)
    packed = packed_ref[...]
    unit = jnp.where(lane < sub, packed, jnp.where(lane == sub, 1.0, 0.0))
    w = jnp.dot(
        held[INV + NB : INV + 2 * NB, :],
        jnp.concatenate([jnp.where(first, -unit, source[:, :NB]), source[:, NB:]], axis=1),
        precision=HIGH, preferred_element_type=F32,
    )
    high = w.astype(BF16)
    right[0:NB, :] = high
    right[NB : 2 * NB, :] = (w - high.astype(F32)).astype(BF16)
    right[2 * NB :, :] = high
    patch[...] = keep(returning_ref[...]) - product(ext[...])

    copies = []
    for j in range(rows // TILE):
        slot = slots.at[j % SLOTS]
        if j >= SLOTS:
            copies[j - SLOTS].wait()
        at = slice(j * TILE, (j + 1) * TILE)
        slot[...] = keep(tile_ref[at, :]) - product(held[at, :])
        if j == 0:
            @pl.when(plane == 0)
            def _():
                upper = jnp.dot(
                    held[INV : INV + NB, :], source, precision=HIGH, preferred_element_type=F32
                )
                slot[0:NB, :] = jnp.concatenate(
                    [jnp.where(first, packed, upper[:, :NB]), upper[:, NB:]], axis=1
                )
        base = plane * rows + j * TILE

        def land(i, carry):
            slot[pl.ds(tab[0, i] - base, 1), :] = patch[pl.ds(i, 1), :]
            return carry

        lax.fori_loop(tab[2, j], tab[2, j + 1], land, 0)
        copies.append(pltpu.make_async_copy(slot, out_ref.at[at, :], sems.at[j % SLOTS]))
        copies[j].start()
    for copy in copies[-SLOTS:]:
        copy.wait()


def update(tile, held, incoming, returning, packed, tab):
    rows, cols = tile.shape
    vmem = pl.BlockSpec(memory_space=pltpu.VMEM)
    return pl.pallas_call(
        update_kernel,
        name="update",
        out_shape=jax.ShapeDtypeStruct((rows, cols), F32),
        in_specs=[pl.BlockSpec(memory_space=pltpu.SMEM)] + [vmem] * 5,
        out_specs=pl.BlockSpec(memory_space=pltpu.HBM),
        scratch_shapes=[
            pltpu.VMEM((SLOTS, TILE, cols), F32),
            pltpu.VMEM((3 * NB, cols), BF16),
            pltpu.VMEM((FEW, cols), F32),
            pltpu.VMEM((FEW, NB), F32),
            pltpu.SemaphoreType.DMA((SLOTS,)),
        ],
        compiler_params=pltpu.CompilerParams(vmem_limit_bytes=24 * 2**20),
    )(tab, tile, held, incoming, returning, packed)


def on_device(matrix, pivot_rows):
    tile, held, incoming, returning, packed, tab = exchange(matrix, pivot_rows)
    return update(tile, held, incoming, returning, packed, tab)


def solution(mesh):
    return jax.shard_map(
        on_device, mesh=mesh, in_specs=(P("prow", "pcol"), P()), out_specs=P("prow", "pcol"), check_vma=False
    )
```

```python
import functools

import jax
import jax.numpy as jnp
from jax import lax
from jax.experimental import pallas as pl
from jax.experimental.pallas import tpu as pltpu
from jax.sharding import PartitionSpec as P

NB = 128
FEW = 96
F32 = jnp.float32
BF16 = jnp.bfloat16
I32 = jnp.int32
HIGH = lax.Precision.HIGHEST
MESH = pl.DeviceIdType.MESH

HOPS = (
    (1, 0, 0), (3, 0, 0), (2, 0, 0), (0, 1, 0), (0, 3, 0), (0, 2, 0),
    (0, 0, 1), (0, 0, 7), (0, 0, 2), (0, 0, 6), (0, 0, 3), (0, 0, 5), (0, 0, 4),
)
FAN = 4
PANEL_TREES = (
    (
        0, 0, 1537, 0, 6367233, 18480, 2060, 14352, 234930336, 624,
        112, 515, 0, 4, 0, 14337, 0, 0, 0, 0,
        12, 196996, 1540, 2052, 4, 515, 0, 4, 0, 0,
        0, 3, 0, 0, 0, 112, 0, 196993, 12, 12,
        513, 1, 513, 0, 3, 0, 0, 16, 112, 1539,
        0, 0, 4, 235078145, 1537, 12, 3, 2049, 4, 0,
        0, 14339, 0, 0, 196993, 12, 0, 0, 79884, 0,
        3, 4, 16, 0, 0, 515, 0, 0, 0, 0,
        0, 0, 112, 262284, 18612609, 25428481, 1837068, 235144708, 0, 262657,
        16, 16, 2050, 0, 14352, 16, 0, 0, 0, 0,
        12, 12, 12, 1, 0, 0, 0, 1, 0, 0,
        0, 0, 0, 0, 12, 0, 12, 12, 1539, 196739,
        515, 4, 0, 0, 0, 112, 0, 0,
    ),
    (
        0, 0, 0, 0, 0, 4, 131, 0, 12, 0,
        12, 0, 34091010, 0, 235089952, 0, 1, 1, 0, 0,
        3, 0, 0, 0, 0, 0, 1539, 14337, 132, 112,
        0, 234946956, 388, 16, 262659, 0, 63489, 112, 0, 0,
        400, 0, 63504, 0, 2294275, 0, 34080260, 112, 0, 0,
        0, 0, 3, 0, 0, 0, 197121, 1540, 12, 0,
        4, 0, 1, 0, 0, 3, 0, 14352, 385, 0,
        0, 0, 263683, 0, 0, 112, 196993, 263684, 197128, 4,
        0, 0, 515, 0, 385, 0, 0, 0, 0, 0,
        385, 0, 4, 0, 17924, 0, 515, 0, 3, 515,
        1837057, 2049, 0, 16, 400, 4, 2051, 0, 235078240, 0,
        30732, 0, 0, 16, 2049, 16, 12, 0, 0, 0,
        528, 0, 1537, 0, 0, 1540, 16899, 0,
    ),
    (
        0, 4, 0, 0, 3, 0, 0, 1648, 0, 0,
        0, 0, 63584, 0, 4, 0, 6488608, 0, 3, 12,
        240, 1, 14352, 0, 3, 1, 16, 12, 1537, 235144705,
        14340, 16, 0, 1, 0, 1, 0, 0, 0, 1,
        0, 12, 0, 0, 0, 17924, 0, 2060, 17411, 197121,
        16, 14340, 0, 528, 0, 63520, 235079683, 0, 16, 3,
        112, 144, 0, 0, 0, 0, 1, 0, 0, 513,
        0, 0, 1539, 0, 0, 12, 112, 4, 0, 3,
        112, 1, 0, 0, 0, 0, 0, 385, 0, 12,
        0, 1, 79875, 197121, 12, 624, 0, 1, 4, 0,
        0, 0, 0, 1, 0, 196993, 0, 1837068, 10224001, 30724,
        0, 67596, 1, 144, 0, 0, 0, 0, 0, 1,
        2049, 263792, 2060, 16, 197121, 1, 12, 4,
    ),
    (
        0, 3933700, 0, 79904, 4, 14416, 0, 132, 0, 0,
        3, 624, 0, 14337, 1552, 0, 0, 3, 0, 4,
        0, 0, 14339, 131, 0, 0, 0, 385, 0, 12,
        8651137, 1, 1537, 262768, 0, 235143681, 0, 0, 0, 18436,
        0, 0, 0, 240, 1, 2060, 12, 0, 12, 0,
        1836548, 33751425, 0, 0, 14339, 2052, 0, 0, 0, 2049,
        16, 0, 2060, 14352, 0, 1, 0, 0, 14348, 1539,
        0, 3, 0, 1835523, 0, 0, 0, 0, 0, 16,
        0, 0, 1, 0, 1540, 234946945, 2360836, 0, 16, 276484,
        235143681, 0, 0, 515, 0, 0, 12, 515, 0, 12,
        0, 3, 1, 0, 0, 0, 0, 0, 0, 0,
        262659, 1539, 524, 14339, 4, 14339, 0, 0, 4, 0,
        0, 0, 3, 1540, 2060, 0, 0, 0,
    ),
    (
        0, 0, 0, 0, 0, 1539, 0, 0, 0, 3,
        2052, 0, 0, 12, 0, 0, 0, 0, 112, 0,
        1, 16, 0, 14348, 0, 0, 0, 0, 14339, 4,
        0, 14348, 112, 396, 112, 0, 624, 0, 112, 79875,
        112, 14337, 0, 0, 112, 14337, 14337, 0, 25231745, 1837057,
        112, 14352, 1835393, 1, 16, 2160, 0, 8128513, 513, 0,
        14337, 12, 0, 0, 0, 2060, 16, 1539, 0, 0,
        16, 2049, 0, 263683, 0, 2051, 0, 2049, 16, 235143308,
        112, 515, 1, 0, 0, 0, 0, 0, 12, 0,
        0, 0, 0, 3, 0, 0, 49284, 196740, 0, 0,
        388, 513, 0, 0, 14340, 0, 14340, 4, 16, 0,
        0, 0, 1835139, 65676, 1540, 262664, 4, 2051, 16, 0,
        0, 0, 63504, 33634307, 0, 16, 0, 0,
    ),
    (
        0, 0, 79904, 235929992, 0, 12, 131, 0, 12, 4,
        3, 2158608, 0, 1, 0, 0, 0, 515, 1, 0,
        0, 0, 0, 0, 33751172, 0, 12, 49312, 112, 0,
        385, 0, 0, 112, 235078147, 0, 0, 2051, 33620353, 112,
        0, 0, 385, 0, 0, 2051, 1835393, 4, 112, 0,
        0, 0, 0, 0, 1, 0, 2049, 0, 0, 513,
        0, 0, 0, 513, 210960, 14340, 235078024, 65667, 14352, 0,
        0, 1, 0, 0, 235144707, 0, 0, 0, 235143553, 0,
        2051, 12, 515, 0, 0, 0, 385, 0, 0, 0,
        0, 14340, 0, 0, 0, 1, 0, 0, 3, 12,
        0, 0, 0, 12, 235078145, 235144708, 263684, 8128001, 0, 0,
        0, 0, 0, 3, 10224096, 1540, 1, 0, 0, 1,
        0, 0, 0, 1, 0, 0, 3, 33572355,
    ),
)
TAIL_TREES = (
    (
        0, 0, 2363404, 0, 1837104, 0, 0, 0, 1839106, 0,
        25223264, 0, 0, 0, 6322224, 0, 0, 112, 196993, 1,
        16899, 0, 0, 112, 513, 0, 0, 0, 0, 0,
        33751425, 0, 0, 0, 6308384, 0, 12, 0, 112, 0,
        8437920, 33751553, 0, 235144708, 16, 0, 0, 0, 0, 0,
        0, 0, 27001217, 1537, 0, 2060, 0, 0, 0, 0,
        0, 0, 25231745, 0, 0, 0, 515, 12, 1537, 0,
        0, 0, 1835393, 0, 0, 0, 1, 0, 0, 0,
        33620364, 0, 0, 235144708, 1835521, 263684, 0, 515, 16, 0,
        0, 0, 1837058, 0, 235078147, 16, 513, 1, 0, 2052,
        0, 0, 0, 0, 0, 0, 197121, 0, 1, 0,
        0, 0, 0, 0, 0, 0, 1, 263681, 0, 0,
        65921, 14340, 0, 2060, 2052, 0, 197121, 0,
    ),
    (
        0, 0, 0, 206896, 1839105, 25231536, 12, 0, 0, 0,
        0, 12, 0, 0, 0, 1836576, 25231490, 12, 1544, 0,
        3, 0, 0, 263684, 112, 0, 235144707, 0, 14348, 1837088,
        112, 0, 0, 0, 0, 1, 513, 235078145, 0, 0,
        0, 0, 0, 0, 0, 0, 0, 235078017, 0, 0,
        235078147, 235143560, 0, 2052, 0, 0, 0, 0, 0, 25231745,
        0, 0, 0, 0, 234948097, 263688, 0, 1539, 14340, 0,
        0, 0, 0, 0, 0, 0, 14338, 0, 0, 0,
        0, 0, 0, 6308360, 0, 0, 0, 14339, 197121, 0,
        0, 1835523, 0, 0, 0, 0, 3670280, 263684, 33751172, 2060,
        0, 14352, 33583106, 0, 1837058, 0, 33603808, 0, 0, 1837059,
        112, 0, 0, 0, 0, 0, 1539, 0, 0, 4,
        513, 0, 0, 0, 0, 0, 0, 3,
    ),
    (
        0, 1544, 0, 235149316, 0, 3, 4, 234946976, 0, 235144752,
        0, 1, 4098, 112, 2144, 0, 0, 0, 1835523, 197123,
        0, 0, 0, 1, 0, 196993, 0, 0, 0, 0,
        0, 1537, 14340, 0, 0, 0, 0, 0, 0, 25231746,
        0, 0, 0, 0, 25231490, 1836548, 197121, 0, 0, 0,
        0, 17924, 0, 0, 0, 385, 0, 25231745, 0, 0,
        0, 0, 0, 33751425, 0, 1836547, 1835144, 0, 0, 0,
        0, 0, 4, 0, 0, 0, 0, 0, 0, 0,
        8406018, 276492, 197232, 0, 235143553, 112, 14352, 1837068, 235143553, 1837057,
        0, 14352, 0, 2051, 14337, 0, 0, 0, 0, 1,
        1, 0, 0, 0, 4, 0, 0, 0, 0, 0,
        197121, 0, 1, 0, 0, 8128001, 0, 0, 0, 385,
        0, 196993, 0, 0, 0, 1, 0, 263681,
    ),
)
TURNS = (
    (
        0, 1417216, 21, 1310720, 4259845, 355206923, 1424, 2969611, 1803, 436207632,
        475268181, 4194320, 20800, 355205141, 4301568, 21, 21504, 7341376, 486645760, 4501504,
        402700053, 486604816, 7426069, 492306448, 65562, 86037, 108352, 7427861, 402698944, 493421568,
        5591040, 493421978, 407110720, 307865408, 402654720, 3235866, 301991296, 1816, 486539293, 407224341,
        402654289, 486645782, 1564, 5767168, 307757846, 410079232, 493356160, 87132, 140034077, 218173464,
        307847168, 222629888, 218105624, 302080018, 409993240, 307847197, 75165, 402655000, 486659933, 7438336,
        225560320, 302080029, 7341568, 5767168, 24, 309593949, 402767872, 301991744, 7604050, 6406144,
        486539293, 409993240, 99864, 494141440, 0, 486659933, 91264, 402769408, 486540864, 410109440,
        486629376, 402767872, 494143325, 24, 6293261, 4718610, 6291480, 118802, 443809792, 6406168,
        7604061, 114712, 70740, 494231552, 116250, 90141, 190055488, 272719872, 116480, 4195712,
        268436893, 357828376, 7602205, 116504, 352322624, 108352, 469763584, 369188893, 436257536, 69632,
        6816896, 5574656, 88145920, 187520768, 272631194, 187434752, 352323349, 268435482, 357826581, 106512,
        66960, 86037, 376022848, 290832384, 5550080, 268502426, 87104, 90112,
    ),
    (
        0, 7077888, 1867, 7188485, 112320, 10358805, 10117136, 8650752, 1873, 8912918,
        2257, 10117132, 7077888, 8650780, 8915072, 135168, 110592, 137692, 10102934, 8653248,
        137280, 0, 0, 10119552, 158102, 10223616, 163862, 17, 135196, 155648,
        162268, 9961472, 10223616, 22, 2257, 163840, 141824, 159772, 2582, 10223644,
        2240, 2560, 28, 2560, 8915456, 10223644, 10485782, 159772, 25, 0,
        163840, 9318400, 2240, 166400, 28, 10488320, 29, 11010048, 0, 172056,
        0, 0, 2688, 10485789, 143380, 10649625, 11012756, 166415, 166425, 0,
        0, 20, 11012736, 0, 26, 0, 166400, 0, 25, 0,
        7866265, 9175068, 9699350, 145600, 9177280, 10488320, 11010076, 10652160, 9865728, 11010048,
        0, 11182104, 2240, 10485760, 11012736, 2589, 121024, 141824, 143381, 10127901,
        10485760, 159744, 163840, 24, 11153432, 29, 174744, 18, 2560, 159744,
        10649600, 0, 9961472, 21, 16, 8650763, 137301, 2432, 0, 10117136,
        166016, 10226112, 0, 2517, 2496, 9961472, 2517, 10117136,
    ),
)
PANEL_ROOT = ((4,), (12,), (16, 12), (1, 3), (48, 112), (3,))
TAIL_ROOT = ((2, 8, 80, 4), (96, 3, 4, 16), (80, 1, 3, 12))
SPREAD = 29
TAIL_SPREAD = 42

TREES = len(PANEL_TREES)
TAILS = len(TAIL_TREES)
PIECE = 32
PANEL = 4096
CHUNKS = tuple(PANEL // PIECE // TREES + (t < PANEL // PIECE % TREES) for t in range(TREES))
MOST = CHUNKS[0]
FIRST = tuple(sum(CHUNKS[:t]) * PIECE for t in range(TREES))
INV = PANEL
TAIL = -(-2 * NB // (8 * TAILS)) * 8
HELD = INV + TAILS * TAIL
SOON = 4
EARLY = 8
TILE = 512


def swap_lists(pivot_col, pivot_row, row_start, tab_ref):
    lane = lax.broadcasted_iota(I32, (NB, NB), 1)
    sub = lax.broadcasted_iota(I32, (NB, NB), 0)
    low = pivot_col >= NB
    smaller = (pivot_row < pivot_col) & (pivot_row >= NB)
    rank = jnp.sum(jnp.where(smaller, 1.0, 0.0), axis=1, keepdims=True)
    lane_f = lane.astype(F32)
    hit = (rank == lane_f) & low
    landing = jnp.sum(jnp.where(hit, pivot_col.astype(F32), 0.0), axis=0, keepdims=True)
    chosen = jnp.sum(jnp.where(pivot_col == lane, 1.0, 0.0), axis=0, keepdims=True)
    free = jnp.broadcast_to(1.0 - chosen, (NB, NB))
    ahead = jnp.sum(jnp.where(lane < sub, free, 0.0), axis=1, keepdims=True)
    own = jnp.sum(jnp.where(lane == sub, free, 0.0), axis=1, keepdims=True)
    place = (ahead == lane_f) & (own > 0.5)
    displaced = jnp.sum(jnp.where(place, sub.astype(F32), 0.0), axis=0, keepdims=True)
    bound = row_start + lane * TILE
    starts = jnp.sum(jnp.where(low & (pivot_col < bound), 1.0, 0.0), axis=0, keepdims=True)
    tab_ref[...] = jnp.concatenate(
        [landing, displaced, starts, jnp.zeros((5, NB), F32)], axis=0
    ).astype(I32)


def pick(values, bits):
    while len(values) > 1:
        bit, bits = bits[0], bits[1:]
        values = [
            lo if isinstance(lo, int) and isinstance(hi, int) and lo == hi else jnp.where(bit, hi, lo)
            for lo, hi in zip(values[::2], values[1::2])
        ]
    return values[0]


def eliminate(
    block, packed_ref, linv_ref, binv_ref, upper_ref, scale_ref, busy_turns, busy, between
):
    lane = lax.broadcasted_iota(I32, (8, NB), 1)
    sub = lax.broadcasted_iota(I32, (8, NB), 0)
    groups = NB // 8
    rows = tuple(block[8 * q : 8 * q + 8, :] for q in range(groups))
    lower = tuple(jnp.zeros((8, NB), F32) for q in range(groups))

    def row_of(x, k):
        return jnp.broadcast_to(x[k : k + 1, :], (8, NB))

    def column_of(x, k):
        return jnp.broadcast_to(x[:, k : k + 1], (8, NB))

    def turn(g, carry, also=None):
        if also is not None:
            also(g)
        a, low = list(carry[0]), list(carry[1])
        seen, scale = a[0], jnp.zeros((8, NB), F32)
        column = [column_of(a[0], j) for j in range(8)]
        for k in range(8):
            pivot = row_of(column[k], k)
            row = row_of(a[0], k)
            inverse = 1.0 / pivot
            here = sub == k
            seen = jnp.where(here, row, seen)
            scale = jnp.where(here, inverse, scale)
            row = jnp.where(lane == k, pivot + 1.0, row)
            first = jnp.where(here, 0.0, column[k] * inverse)
            for j in range(k + 1, 8):
                column[j] = column[j] - first * row_of(column[j], k)
            kept = lane == 8 * g + k
            for q in range(groups):
                factor = first if q == 0 else column_of(a[q], k) * inverse
                a[q] = a[q] - factor * row
                low[q] = jnp.where(kept, factor, low[q])
            a[0] = jnp.where(here & (lane == k), 1.0, a[0])
        at = pl.ds(pl.multiple_of(8 * g, 8), 8)
        upper_ref[at, :] = seen
        scale_ref[at, :] = scale
        a = [pltpu.roll(x, NB - 8, 1) for x in a]
        return tuple(a[1:] + a[:1]), tuple(low[1:] + low[:1])

    carry = lax.fori_loop(0, busy_turns, functools.partial(turn, also=busy), (rows, lower))
    between()
    rows, lower = lax.fori_loop(busy_turns, groups, turn, carry)
    for q in range(groups):
        at = slice(8 * q, 8 * q + 8)
        seen = upper_ref[at, :]
        if q:
            seen = pltpu.roll(seen, 8 * q, 1)
        below = lane < sub + 8 * q
        packed_ref[at, :] = jnp.where(below, lower[q], seen)
        linv_ref[at, :] = jnp.where(below, seen, jnp.where(lane == sub + 8 * q, 1.0, 0.0))
        binv_ref[at, :] = rows[q] * scale_ref[at, :]


def exchange_kernel(
    pivots, matrix, tile_ref, held, returning_ref, right, top, tab_ref,
    incoming_ref, packed_ref, rows_ref, other, linv_ref, upper_ref, scale_ref, pivots_v, pivots_sm, tab_sm,
    arrive, depart, tail_arrive, tail_depart, root_depart, swap_sems, local_sems,
):
    plane, chip = lax.axis_index("prow"), lax.axis_index("pcol")
    rows_dev, cols = matrix.shape
    row_start = plane * rows_dev
    root = chip == 0

    fetch_sm = pltpu.make_async_copy(pivots, pivots_sm, local_sems.at[2])
    fetch_v = pltpu.make_async_copy(pivots, pivots_v, local_sems.at[3])
    fetch_v.start()
    fetch_sm.start()

    @pl.when(root)
    def _():
        for c in range(MOST):
            for t in range(TREES):
                if c < CHUNKS[t]:
                    lo = FIRST[t] + c * PIECE
                    pltpu.make_async_copy(
                        matrix.at[pl.ds(lo, PIECE), pl.ds(0, NB)],
                        held.at[pl.ds(lo, PIECE), :],
                        arrive.at[t, c],
                    ).start()
    load = pltpu.make_async_copy(matrix, tile_ref, local_sems.at[0])
    load.start()

    x, y, z = chip % 4, (chip // 4) % 4, chip // 16
    barrier = pltpu.get_barrier_semaphore()
    for dx, dy, dz in HOPS:
        there = (x + dx) % 4 + 4 * ((y + dy) % 4) + 16 * ((z + dz) % 8)
        pl.semaphore_signal(barrier, inc=1, device_id=(plane, there), device_id_type=MESH)
    pl.semaphore_signal(barrier, inc=1, device_id=(1 - plane, chip), device_id_type=MESH)

    fetch_v.wait()
    pivot_row = jnp.broadcast_to(pivots_v[...], (NB, NB))
    pivot_col = jnp.transpose(pivot_row.astype(F32)).astype(I32)
    swap_lists(pivot_col, pivot_row, row_start, tab_ref)
    move = pltpu.make_async_copy(tab_ref, tab_sm, local_sems.at[1])
    move.start()
    mine = (pivot_col >= row_start) & (pivot_col < row_start + rows_dev)

    def gather_pivots():
        fetch_sm.wait()
        load.wait()

        def some(i, carry):
            for j in range(8):
                k = 8 * i + j
                local = jnp.clip(pivots_sm[0, k] - row_start, 0, rows_dev - 1)
                rows_ref[pl.ds(k, 1), :] = tile_ref[pl.ds(local, 1), :]
            return carry

        lax.fori_loop(0, NB // 8, some, 0)
        swaps[0].start()
        swaps[1].start()

    def swap_of(i, rows, columns):
        return pltpu.make_async_remote_copy(
            src_ref=rows_ref.at[rows, columns], dst_ref=other.at[rows, columns],
            send_sem=swap_sems.at[i, 0], recv_sem=swap_sems.at[i, 1],
            device_id=(1 - plane, chip), device_id_type=MESH,
        )

    swaps = [
        swap_of(0, pl.ds(0, NB), pl.ds(0, NB)),
        swap_of(1, pl.ds(0, NB), pl.ds(NB, cols - NB)),
        swap_of(2, pl.ds(NB, FEW), pl.ds(0, cols)),
    ]

    def gather_displaced():
        move.wait()

        def some(i, carry):
            for j in range(8):
                k = 8 * i + j
                local = jnp.clip(tab_sm[1, k], 0, NB - 1)
                rows_ref[pl.ds(NB + k, 1), :] = tile_ref[pl.ds(local, 1), :]
            return carry

        lax.fori_loop(0, FEW // 8, some, 0)
        swaps[2].start()

    def merge(at):
        incoming_ref[:, at] = jnp.where(mine, rows_ref[:NB, at], other[:NB, at])

    def merge_rest():
        for j in range(1, cols // NB):
            merge(slice(j * NB, (j + 1) * NB))
        returning_ref[...] = jnp.where(plane == 0, rows_ref[NB:, :], other[NB:, :])

    def prepare():
        source = incoming_ref[...]
        lane = lax.broadcasted_iota(I32, (NB, NB), 1)
        sub = lax.broadcasted_iota(I32, (NB, NB), 0)
        packed = packed_ref[...]
        unit = jnp.where(lane < sub, packed, jnp.where(lane == sub, 1.0, 0.0))
        w = jnp.dot(
            held[INV + NB : INV + 2 * NB, :],
            jnp.concatenate([jnp.where(root, -unit, source[:, :NB]), source[:, NB:]], axis=1),
            precision=HIGH, preferred_element_type=F32,
        )
        high = w.astype(BF16)
        right[0:NB, :] = high
        right[NB : 2 * NB, :] = (w - high.astype(F32)).astype(BF16)
        right[2 * NB :, :] = high

        @pl.when(plane == 0)
        def _():
            upper = jnp.dot(
                held[INV : INV + NB, :], source, precision=HIGH, preferred_element_type=F32
            )
            top[...] = jnp.concatenate(
                [jnp.where(root, packed, upper[:, :NB]), upper[:, NB:]], axis=1
            )

    def arrived(at, sem):
        pltpu.make_async_copy(held.at[at, :], held.at[at, :], sem).wait()

    def send(at, out_sem, in_sem, there):
        pltpu.make_async_remote_copy(
            src_ref=held.at[at, :], dst_ref=held.at[at, :], send_sem=out_sem, recv_sem=in_sem,
            device_id=(plane, there), device_id_type=MESH,
        ).start()

    def piece(t, c):
        return pl.ds(pl.multiple_of(FIRST[t] + c * PIECE, 8), PIECE)

    def tail(t):
        return pl.ds(INV + t * TAIL, TAIL)

    def offset(code):
        dx, dy, dz = code % 4, (code // 4) % 4, code // 16
        mirror = (4 - dx) % 4 + 4 * ((4 - dy) % 4) + 16 * ((8 - dz) % 8)
        return jnp.where(plane == 0, code, mirror)

    def steps(word):
        return [(word // 128**i) % 128 for i in range(FAN)]

    @pl.when(root)
    def _():
        def spread(c, trees=range(TREES)):
            for t in trees:
                at = piece(t, c)
                for i, code in enumerate(PANEL_ROOT[t]):
                    send(at, root_depart.at[t, i], arrive.at[t, c], offset(code))

        def staged(c):
            for t in range(TREES):
                if c < CHUNKS[t]:
                    arrived(piece(t, c), arrive.at[t, c])

        pl.semaphore_wait(barrier, len(HOPS) + 1)
        for c in range(SOON):
            staged(c)
            spread(c)
        gather_pivots()
        gather_displaced()
        for c in range(SOON, MOST):
            staged(c)
        for c in range(SOON, EARLY):
            spread(c)
        swaps[0].wait()
        merge(slice(0, NB))
        eliminate(
            incoming_ref[:, :NB], packed_ref, linv_ref, held.at[INV + NB : INV + 2 * NB, :],
            upper_ref, scale_ref, CHUNKS[-1] - EARLY, lambda g: spread(g + EARLY),
            lambda: spread(MOST - 1, [t for t in range(TREES) if CHUNKS[t] == MOST]),
        )
        swaps[1].wait()
        swaps[2].wait()
        held[INV : INV + NB, :] = linv_ref[...]

        @pl.when(plane == 1)
        def _():
            held[INV : INV + FEW, :] = other[NB:, :NB]

        if HELD > INV + 2 * NB:
            held[INV + 2 * NB : HELD, :] = jnp.zeros((HELD - INV - 2 * NB, NB), F32)
        for t in range(TAILS):
            for i, code in enumerate(TAIL_ROOT[t]):
                send(tail(t), root_depart.at[TREES + t, i], tail_arrive.at[t], offset(code))
        merge_rest()
        prepare()
        for t in range(TREES + TAILS):
            for i in range(len((PANEL_ROOT + TAIL_ROOT)[t])):
                at = pl.ds(0, CHUNKS[t] * PIECE if t < TREES else TAIL)
                arrived(at, root_depart.at[t, i])

    @pl.when(chip != 0)
    def _():
        place = jnp.where(plane == 0, chip, (4 - x) % 4 + 4 * ((4 - y) % 4) + 16 * ((8 - z) % 8))
        bits = [(place // (2**i)) % 2 == 1 for i in range(7)]

        def chips_of(word):
            codes, there = steps(word), []
            for code in codes:
                dx, dy, dz = code % 4, (code // 4) % 4, code // 16
                sign = 1 - 2 * plane
                there.append(
                    (x + sign * dx + 4) % 4 + 4 * ((y + sign * dy + 4) % 4)
                    + 16 * ((z + sign * dz + 8) % 8)
                )
            return codes, there

        panel = [chips_of(pick(list(table), bits)) for table in PANEL_TREES]
        turn_words = [pick(list(table), bits) for table in TURNS]
        turns = [(turn_words[t // 5] // 64 ** (t % 5)) % 64 for t in range(TREES + TAILS)]
        tails = [chips_of(pick(list(table), bits)) for table in TAIL_TREES]
        pl.semaphore_wait(barrier, len(HOPS) + 1)
        gather_pivots()
        gather_displaced()

        def send_all(node, at, out_sems, in_sem):
            codes, there = node
            send(at, out_sems.at[0], in_sem, there[0])

            @pl.when(codes[1] > 0)
            def _():
                send(at, out_sems.at[1], in_sem, there[1])

                @pl.when(codes[2] > 0)
                def _():
                    send(at, out_sems.at[2], in_sem, there[2])

                    @pl.when(codes[3] > 0)
                    def _():
                        send(at, out_sems.at[3], in_sem, there[3])

        def pass_on(s, carry):
            for t in range(TREES):
                c = s - turns[t]

                @pl.when((c >= 0) & (c < CHUNKS[t]) & (panel[t][0][0] > 0))
                def _():
                    at = piece(t, c)
                    arrived(at, arrive.at[t, c])
                    send_all(panel[t], at, depart.at[t], arrive.at[t, c])
            for t in range(TAILS):
                @pl.when((turns[TREES + t] == s) & (tails[t][0][0] > 0))
                def _():
                    arrived(tail(t), tail_arrive.at[t])
                    send_all(tails[t], tail(t), tail_depart.at[t], tail_arrive.at[t])
            return carry

        lax.fori_loop(1, max(SPREAD + MOST, TAIL_SPREAD + 1), pass_on, 0)
        for swap in swaps:
            swap.wait()
        merge(slice(0, NB))
        merge_rest()

        for t in range(TAILS):
            @pl.when(tails[t][0][0] == 0)
            def _():
                arrived(tail(t), tail_arrive.at[t])
        prepare()
        for t in range(TREES):
            @pl.when(panel[t][0][0] == 0)
            def _():
                for c in range(CHUNKS[t]):
                    arrived(piece(t, c), arrive.at[t, c])
        for t in range(TREES + TAILS):
            codes = (panel + tails)[t][0]
            for i in range(FAN):
                @pl.when(codes[i] > 0)
                def _():
                    if t < TREES:
                        arrived(pl.ds(0, CHUNKS[t] * PIECE), depart.at[t, i])
                    else:
                        arrived(pl.ds(0, TAIL), tail_depart.at[t - TREES, i])


def exchange(matrix, pivot_rows):
    rows, cols = matrix.shape
    vmem = pl.BlockSpec(memory_space=pltpu.VMEM)
    return pl.pallas_call(
        exchange_kernel,
        name="exchange",
        out_shape=(
            jax.ShapeDtypeStruct((rows, cols), F32),
            jax.ShapeDtypeStruct((HELD, NB), F32),
            jax.ShapeDtypeStruct((FEW, cols), F32),
            jax.ShapeDtypeStruct((3 * NB, cols), BF16),
            jax.ShapeDtypeStruct((NB, cols), F32),
            jax.ShapeDtypeStruct((8, NB), I32),
        ),
        in_specs=[pl.BlockSpec(memory_space=pltpu.HBM)] * 2,
        out_specs=(vmem,) * 6,
        scratch_shapes=[
            pltpu.VMEM((NB, cols), F32),
            pltpu.VMEM((NB, NB), F32),
            pltpu.VMEM((NB + FEW, cols), F32),
            pltpu.VMEM((NB + FEW, cols), F32),
            pltpu.VMEM((NB, NB), F32),
            pltpu.VMEM((NB, NB), F32),
            pltpu.VMEM((NB, NB), F32),
            pltpu.VMEM((1, NB), I32),
            pltpu.SMEM((1, NB), I32),
            pltpu.SMEM((8, NB), I32),
            pltpu.SemaphoreType.DMA((TREES, MOST)),
            pltpu.SemaphoreType.DMA((TREES, FAN)),
            pltpu.SemaphoreType.DMA((TAILS,)),
            pltpu.SemaphoreType.DMA((TAILS, FAN)),
            pltpu.SemaphoreType.DMA((TREES + TAILS, max(map(len, PANEL_ROOT + TAIL_ROOT)))),
            pltpu.SemaphoreType.DMA((3, 2)),
            pltpu.SemaphoreType.DMA((4,)),
        ],
        compiler_params=pltpu.CompilerParams(
            collective_id=0, has_side_effects=True, vmem_limit_bytes=44 * 2**20
        ),
    )(pivot_rows.reshape(1, NB), matrix)


SLOTS = 3


def update_kernel(
    tab, tile_ref, held, returning_ref, right, top, out_ref, slots, patch, ext, sems,
):
    plane, first = lax.axis_index("prow"), lax.axis_index("pcol") == 0
    rows = tile_ref.shape[0]

    def product(left_f32):
        high = left_f32.astype(BF16)
        low = (left_f32 - high.astype(F32)).astype(BF16)
        return jnp.dot(
            jnp.concatenate([high, high, low], axis=1), right[...], preferred_element_type=F32
        )

    def keep(block):
        return jnp.concatenate([jnp.where(first, 0.0, block[:, :NB]), block[:, NB:]], axis=1)

    @pl.when(plane == 1)
    def _():
        ext[...] = held[INV : INV + FEW, :]

    @pl.when(plane == 0)
    def _():
        def take(i, carry):
            for k in range(8):
                row = jnp.clip(tab[1, 8 * i + k], 0, NB - 1)
                ext[pl.ds(8 * i + k, 1), :] = held[pl.ds(row, 1), :]
            return carry

        lax.fori_loop(0, FEW // 8, take, 0)

    patch[...] = keep(returning_ref[...]) - product(ext[...])

    copies = []
    for j in range(rows // TILE):
        slot = slots.at[j % SLOTS]
        if j >= SLOTS:
            copies[j - SLOTS].wait()
        at = slice(j * TILE, (j + 1) * TILE)
        slot[...] = keep(tile_ref[at, :]) - product(held[at, :])
        if j == 0:
            @pl.when(plane == 0)
            def _():
                slot[0:NB, :] = top[...]
        base = plane * rows + j * TILE

        def land(i, carry):
            slot[pl.ds(tab[0, i] - base, 1), :] = patch[pl.ds(i, 1), :]
            return carry

        lax.fori_loop(tab[2, j], tab[2, j + 1], land, 0)
        copies.append(pltpu.make_async_copy(slot, out_ref.at[at, :], sems.at[j % SLOTS]))
        copies[j].start()
    for copy in copies[-SLOTS:]:
        copy.wait()


def update(tile, held, returning, right, top, tab):
    rows, cols = tile.shape
    vmem = pl.BlockSpec(memory_space=pltpu.VMEM)
    return pl.pallas_call(
        update_kernel,
        name="update",
        out_shape=jax.ShapeDtypeStruct((rows, cols), F32),
        in_specs=[pl.BlockSpec(memory_space=pltpu.SMEM)] + [vmem] * 5,
        out_specs=pl.BlockSpec(memory_space=pltpu.HBM),
        scratch_shapes=[
            pltpu.VMEM((SLOTS, TILE, cols), F32),
            pltpu.VMEM((FEW, cols), F32),
            pltpu.VMEM((FEW, NB), F32),
            pltpu.SemaphoreType.DMA((SLOTS,)),
        ],
        compiler_params=pltpu.CompilerParams(vmem_limit_bytes=24 * 2**20),
    )(tab, tile, held, returning, right, top)


def on_device(matrix, pivot_rows):
    return update(*exchange(matrix, pivot_rows))


def solution(mesh):
    return jax.shard_map(
        on_device, mesh=mesh, in_specs=(P("prow", "pcol"), P()), out_specs=P("prow", "pcol"), check_vma=False
    )
```

```python
import functools

import jax
import jax.numpy as jnp
from jax import lax
from jax.experimental import pallas as pl
from jax.experimental.pallas import tpu as pltpu
from jax.sharding import PartitionSpec as P

NB = 128
FEW = 96
F32 = jnp.float32
BF16 = jnp.bfloat16
I32 = jnp.int32
HIGH = lax.Precision.HIGHEST
MESH = pl.DeviceIdType.MESH

HOPS = (
    (1, 0, 0), (3, 0, 0), (2, 0, 0), (0, 1, 0), (0, 3, 0), (0, 2, 0),
    (0, 0, 1), (0, 0, 7), (0, 0, 2), (0, 0, 6), (0, 0, 3), (0, 0, 5), (0, 0, 4),
)
FAN = 4
PANEL_TREES = (
    (
        0, 0, 1537, 0, 6367233, 18480, 2060, 14352, 234930336, 624,
        112, 515, 0, 4, 0, 14337, 0, 0, 0, 0,
        12, 196996, 1540, 2052, 4, 515, 0, 4, 0, 0,
        0, 3, 0, 0, 0, 112, 0, 196993, 12, 12,
        513, 1, 513, 0, 3, 0, 0, 16, 112, 1539,
        0, 0, 4, 235078145, 1537, 12, 3, 2049, 4, 0,
        0, 14339, 0, 0, 196993, 12, 0, 0, 79884, 0,
        3, 4, 16, 0, 0, 515, 0, 0, 0, 0,
        0, 0, 112, 262284, 18612609, 25428481, 1837068, 235144708, 0, 262657,
        16, 16, 2050, 0, 14352, 16, 0, 0, 0, 0,
        12, 12, 12, 1, 0, 0, 0, 1, 0, 0,
        0, 0, 0, 0, 12, 0, 12, 12, 1539, 196739,
        515, 4, 0, 0, 0, 112, 0, 0,
    ),
    (
        0, 0, 0, 0, 0, 4, 131, 0, 12, 0,
        12, 0, 34091010, 0, 235089952, 0, 1, 1, 0, 0,
        3, 0, 0, 0, 0, 0, 1539, 14337, 132, 112,
        0, 234946956, 388, 16, 262659, 0, 63489, 112, 0, 0,
        400, 0, 63504, 0, 2294275, 0, 34080260, 112, 0, 0,
        0, 0, 3, 0, 0, 0, 197121, 1540, 12, 0,
        4, 0, 1, 0, 0, 3, 0, 14352, 385, 0,
        0, 0, 263683, 0, 0, 112, 196993, 263684, 197128, 4,
        0, 0, 515, 0, 385, 0, 0, 0, 0, 0,
        385, 0, 4, 0, 17924, 0, 515, 0, 3, 515,
        1837057, 2049, 0, 16, 400, 4, 2051, 0, 235078240, 0,
        30732, 0, 0, 16, 2049, 16, 12, 0, 0, 0,
        528, 0, 1537, 0, 0, 1540, 16899, 0,
    ),
    (
        0, 4, 0, 0, 3, 0, 0, 1648, 0, 0,
        0, 0, 63584, 0, 4, 0, 6488608, 0, 3, 12,
        240, 1, 14352, 0, 3, 1, 16, 12, 1537, 235144705,
        14340, 16, 0, 1, 0, 1, 0, 0, 0, 1,
        0, 12, 0, 0, 0, 17924, 0, 2060, 17411, 197121,
        16, 14340, 0, 528, 0, 63520, 235079683, 0, 16, 3,
        112, 144, 0, 0, 0, 0, 1, 0, 0, 513,
        0, 0, 1539, 0, 0, 12, 112, 4, 0, 3,
        112, 1, 0, 0, 0, 0, 0, 385, 0, 12,
        0, 1, 79875, 197121, 12, 624, 0, 1, 4, 0,
        0, 0, 0, 1, 0, 196993, 0, 1837068, 10224001, 30724,
        0, 67596, 1, 144, 0, 0, 0, 0, 0, 1,
        2049, 263792, 2060, 16, 197121, 1, 12, 4,
    ),
    (
        0, 3933700, 0, 79904, 4, 14416, 0, 132, 0, 0,
        3, 624, 0, 14337, 1552, 0, 0, 3, 0, 4,
        0, 0, 14339, 131, 0, 0, 0, 385, 0, 12,
        8651137, 1, 1537, 262768, 0, 235143681, 0, 0, 0, 18436,
        0, 0, 0, 240, 1, 2060, 12, 0, 12, 0,
        1836548, 33751425, 0, 0, 14339, 2052, 0, 0, 0, 2049,
        16, 0, 2060, 14352, 0, 1, 0, 0, 14348, 1539,
        0, 3, 0, 1835523, 0, 0, 0, 0, 0, 16,
        0, 0, 1, 0, 1540, 234946945, 2360836, 0, 16, 276484,
        235143681, 0, 0, 515, 0, 0, 12, 515, 0, 12,
        0, 3, 1, 0, 0, 0, 0, 0, 0, 0,
        262659, 1539, 524, 14339, 4, 14339, 0, 0, 4, 0,
        0, 0, 3, 1540, 2060, 0, 0, 0,
    ),
    (
        0, 0, 0, 0, 0, 1539, 0, 0, 0, 3,
        2052, 0, 0, 12, 0, 0, 0, 0, 112, 0,
        1, 16, 0, 14348, 0, 0, 0, 0, 14339, 4,
        0, 14348, 112, 396, 112, 0, 624, 0, 112, 79875,
        112, 14337, 0, 0, 112, 14337, 14337, 0, 25231745, 1837057,
        112, 14352, 1835393, 1, 16, 2160, 0, 8128513, 513, 0,
        14337, 12, 0, 0, 0, 2060, 16, 1539, 0, 0,
        16, 2049, 0, 263683, 0, 2051, 0, 2049, 16, 235143308,
        112, 515, 1, 0, 0, 0, 0, 0, 12, 0,
        0, 0, 0, 3, 0, 0, 49284, 196740, 0, 0,
        388, 513, 0, 0, 14340, 0, 14340, 4, 16, 0,
        0, 0, 1835139, 65676, 1540, 262664, 4, 2051, 16, 0,
        0, 0, 63504, 33634307, 0, 16, 0, 0,
    ),
    (
        0, 0, 79904, 235929992, 0, 12, 131, 0, 12, 4,
        3, 2158608, 0, 1, 0, 0, 0, 515, 1, 0,
        0, 0, 0, 0, 33751172, 0, 12, 49312, 112, 0,
        385, 0, 0, 112, 235078147, 0, 0, 2051, 33620353, 112,
        0, 0, 385, 0, 0, 2051, 1835393, 4, 112, 0,
        0, 0, 0, 0, 1, 0, 2049, 0, 0, 513,
        0, 0, 0, 513, 210960, 14340, 235078024, 65667, 14352, 0,
        0, 1, 0, 0, 235144707, 0, 0, 0, 235143553, 0,
        2051, 12, 515, 0, 0, 0, 385, 0, 0, 0,
        0, 14340, 0, 0, 0, 1, 0, 0, 3, 12,
        0, 0, 0, 12, 235078145, 235144708, 263684, 8128001, 0, 0,
        0, 0, 0, 3, 10224096, 1540, 1, 0, 0, 1,
        0, 0, 0, 1, 0, 0, 3, 33572355,
    ),
)
TAIL_TREES = (
    (
        0, 0, 2363404, 0, 1837104, 0, 0, 0, 1839106, 0,
        25223264, 0, 0, 0, 6322224, 0, 0, 112, 196993, 1,
        16899, 0, 0, 112, 513, 0, 0, 0, 0, 0,
        33751425, 0, 0, 0, 6308384, 0, 12, 0, 112, 0,
        8437920, 33751553, 0, 235144708, 16, 0, 0, 0, 0, 0,
        0, 0, 27001217, 1537, 0, 2060, 0, 0, 0, 0,
        0, 0, 25231745, 0, 0, 0, 515, 12, 1537, 0,
        0, 0, 1835393, 0, 0, 0, 1, 0, 0, 0,
        33620364, 0, 0, 235144708, 1835521, 263684, 0, 515, 16, 0,
        0, 0, 1837058, 0, 235078147, 16, 513, 1, 0, 2052,
        0, 0, 0, 0, 0, 0, 197121, 0, 1, 0,
        0, 0, 0, 0, 0, 0, 1, 263681, 0, 0,
        65921, 14340, 0, 2060, 2052, 0, 197121, 0,
    ),
    (
        0, 0, 0, 206896, 1839105, 25231536, 12, 0, 0, 0,
        0, 12, 0, 0, 0, 1836576, 25231490, 12, 1544, 0,
        3, 0, 0, 263684, 112, 0, 235144707, 0, 14348, 1837088,
        112, 0, 0, 0, 0, 1, 513, 235078145, 0, 0,
        0, 0, 0, 0, 0, 0, 0, 235078017, 0, 0,
        235078147, 235143560, 0, 2052, 0, 0, 0, 0, 0, 25231745,
        0, 0, 0, 0, 234948097, 263688, 0, 1539, 14340, 0,
        0, 0, 0, 0, 0, 0, 14338, 0, 0, 0,
        0, 0, 0, 6308360, 0, 0, 0, 14339, 197121, 0,
        0, 1835523, 0, 0, 0, 0, 3670280, 263684, 33751172, 2060,
        0, 14352, 33583106, 0, 1837058, 0, 33603808, 0, 0, 1837059,
        112, 0, 0, 0, 0, 0, 1539, 0, 0, 4,
        513, 0, 0, 0, 0, 0, 0, 3,
    ),
    (
        0, 1544, 0, 235149316, 0, 3, 4, 234946976, 0, 235144752,
        0, 1, 4098, 112, 2144, 0, 0, 0, 1835523, 197123,
        0, 0, 0, 1, 0, 196993, 0, 0, 0, 0,
        0, 1537, 14340, 0, 0, 0, 0, 0, 0, 25231746,
        0, 0, 0, 0, 25231490, 1836548, 197121, 0, 0, 0,
        0, 17924, 0, 0, 0, 385, 0, 25231745, 0, 0,
        0, 0, 0, 33751425, 0, 1836547, 1835144, 0, 0, 0,
        0, 0, 4, 0, 0, 0, 0, 0, 0, 0,
        8406018, 276492, 197232, 0, 235143553, 112, 14352, 1837068, 235143553, 1837057,
        0, 14352, 0, 2051, 14337, 0, 0, 0, 0, 1,
        1, 0, 0, 0, 4, 0, 0, 0, 0, 0,
        197121, 0, 1, 0, 0, 8128001, 0, 0, 0, 385,
        0, 196993, 0, 0, 0, 1, 0, 263681,
    ),
)
TURNS = (
    (
        0, 1970176, 26, 1835008, 5324807, 439617741, 1812, 3514381, 2253, 553648148,
        594019674, 5242900, 29120, 439615514, 5379008, 26, 29952, 9176704, 604114944, 5558272,
        503371994, 604061716, 9281562, 611319828, 81953, 106522, 137472, 9283802, 503370560, 612713728,
        6922240, 612714273, 508822848, 393353472, 503318400, 4046881, 385877760, 2270, 603979812, 508964890,
        503317845, 604114972, 1955, 7340032, 393216988, 512598016, 612632000, 107875, 175173668, 285298718,
        393330688, 290803712, 285214942, 385990679, 512491550, 393330724, 96036, 503318750, 604129572, 9297920,
        294533312, 385990692, 9176960, 7340032, 30, 395315492, 503459840, 385878272, 9439511, 8007680,
        603979812, 512491550, 124830, 613416960, 0, 604129572, 116160, 503461760, 603981760, 512636800,
        604094464, 503459840, 613419300, 30, 7866577, 6029335, 7864350, 147479, 563085312, 8007710,
        9439524, 143390, 87385, 613531648, 145313, 114724, 224920896, 340901888, 145600, 5244672,
        335546148, 443025630, 9437220, 145630, 436208960, 137472, 587204480, 469876772, 553710528, 86016,
        8652224, 6901760, 122765312, 221620416, 340789025, 221513920, 436209882, 335544353, 443023386, 135188,
        83732, 106522, 478550272, 359280640, 6868992, 335628065, 107840, 114688,
    ),
    (
        0, 8912896, 2253, 9052167, 141440, 12746778, 12513300, 10485760, 2261, 11010076,
        2837, 12513295, 8912896, 10485795, 11012736, 163840, 139264, 166947, 12495516, 10488832,
        166400, 0, 0, 12516288, 195548, 12582912, 204828, 21, 163875, 192512,
        199715, 12320768, 12582912, 28, 2837, 204800, 175232, 196643, 3228, 12582947,
        2816, 3200, 35, 3200, 11013248, 12582947, 13107228, 196643, 31, 0,
        204800, 11714560, 2816, 208000, 35, 13110400, 36, 13631488, 0, 213022,
        0, 0, 3328, 13107236, 180249, 13312031, 13634841, 208018, 208031, 0,
        0, 25, 13634816, 0, 33, 0, 208000, 0, 31, 0,
        9701727, 11534371, 11796508, 183040, 11537152, 13110400, 13631523, 13315200, 12004480, 13631488,
        0, 13844510, 2816, 13107200, 13634816, 3236, 146176, 175232, 180250, 12528804,
        13107200, 196608, 204800, 30, 13811742, 36, 216350, 23, 3200, 196608,
        13312000, 0, 12320768, 26, 20, 10485773, 166426, 3008, 0, 12513300,
        207488, 12585984, 0, 3098, 3072, 12320768, 3098, 12513300,
    ),
)
PANEL_ROOT = ((4,), (12,), (16, 12), (1, 3), (48, 112), (3,))
TAIL_ROOT = ((2, 8, 80, 4), (96, 3, 4, 16), (80, 1, 3, 12))
SPREAD = 36
TAIL_SPREAD = 52

TREES = len(PANEL_TREES)
TAILS = len(TAIL_TREES)
PIECE = 32
PANEL = 4096
CHUNKS = tuple(PANEL // PIECE // TREES + (t < PANEL // PIECE % TREES) for t in range(TREES))
MOST = CHUNKS[0]
FIRST = tuple(sum(CHUNKS[:t]) * PIECE for t in range(TREES))
INV = PANEL
TAIL = -(-2 * NB // (8 * TAILS)) * 8
HELD = INV + TAILS * TAIL
SOON = 4
EARLY = 8
TILE = 512


def swap_lists(pivot_col, pivot_row, row_start, tab_ref):
    lane = lax.broadcasted_iota(I32, (NB, NB), 1)
    sub = lax.broadcasted_iota(I32, (NB, NB), 0)
    low = pivot_col >= NB
    smaller = (pivot_row < pivot_col) & (pivot_row >= NB)
    rank = jnp.sum(jnp.where(smaller, 1.0, 0.0), axis=1, keepdims=True)
    lane_f = lane.astype(F32)
    hit = (rank == lane_f) & low
    landing = jnp.sum(jnp.where(hit, pivot_col.astype(F32), 0.0), axis=0, keepdims=True)
    chosen = jnp.sum(jnp.where(pivot_col == lane, 1.0, 0.0), axis=0, keepdims=True)
    free = jnp.broadcast_to(1.0 - chosen, (NB, NB))
    ahead = jnp.sum(jnp.where(lane < sub, free, 0.0), axis=1, keepdims=True)
    own = jnp.sum(jnp.where(lane == sub, free, 0.0), axis=1, keepdims=True)
    place = (ahead == lane_f) & (own > 0.5)
    displaced = jnp.sum(jnp.where(place, sub.astype(F32), 0.0), axis=0, keepdims=True)
    bound = row_start + lane * TILE
    starts = jnp.sum(jnp.where(low & (pivot_col < bound), 1.0, 0.0), axis=0, keepdims=True)
    tab_ref[...] = jnp.concatenate(
        [landing, displaced, starts, jnp.zeros((5, NB), F32)], axis=0
    ).astype(I32)


def pick(values, bits):
    while len(values) > 1:
        bit, bits = bits[0], bits[1:]
        values = [
            lo if isinstance(lo, int) and isinstance(hi, int) and lo == hi else jnp.where(bit, hi, lo)
            for lo, hi in zip(values[::2], values[1::2])
        ]
    return values[0]


def eliminate(
    block, packed_ref, linv_ref, binv_ref, upper_ref, scale_ref, busy_turns, busy, between
):
    lane = lax.broadcasted_iota(I32, (8, NB), 1)
    sub = lax.broadcasted_iota(I32, (8, NB), 0)
    groups = NB // 8
    rows = tuple(block[8 * q : 8 * q + 8, :] for q in range(groups))
    lower = tuple(jnp.zeros((8, NB), F32) for q in range(groups))

    def row_of(x, k):
        return jnp.broadcast_to(x[k : k + 1, :], (8, NB))

    def column_of(x, k):
        return jnp.broadcast_to(x[:, k : k + 1], (8, NB))

    def turn(g, carry, also=None):
        if also is not None:
            also(g)
        a, low = list(carry[0]), list(carry[1])
        seen, scale = a[0], jnp.zeros((8, NB), F32)
        column = [column_of(a[0], j) for j in range(8)]
        for k in range(8):
            pivot = row_of(column[k], k)
            row = row_of(a[0], k)
            inverse = 1.0 / pivot
            here = sub == k
            seen = jnp.where(here, row, seen)
            scale = jnp.where(here, inverse, scale)
            row = jnp.where(lane == k, pivot + 1.0, row)
            first = jnp.where(here, 0.0, column[k] * inverse)
            for j in range(k + 1, 8):
                column[j] = column[j] - first * row_of(column[j], k)
            kept = lane == 8 * g + k
            for q in range(groups):
                factor = first if q == 0 else column_of(a[q], k) * inverse
                a[q] = a[q] - factor * row
                low[q] = jnp.where(kept, factor, low[q])
            a[0] = jnp.where(here & (lane == k), 1.0, a[0])
        at = pl.ds(pl.multiple_of(8 * g, 8), 8)
        upper_ref[at, :] = seen
        scale_ref[at, :] = scale
        a = [pltpu.roll(x, NB - 8, 1) for x in a]
        return tuple(a[1:] + a[:1]), tuple(low[1:] + low[:1])

    carry = lax.fori_loop(0, busy_turns, functools.partial(turn, also=busy), (rows, lower))
    between()
    rows, lower = lax.fori_loop(busy_turns, groups, turn, carry)
    for q in range(groups):
        at = slice(8 * q, 8 * q + 8)
        seen = upper_ref[at, :]
        if q:
            seen = pltpu.roll(seen, 8 * q, 1)
        below = lane < sub + 8 * q
        packed_ref[at, :] = jnp.where(below, lower[q], seen)
        linv_ref[at, :] = jnp.where(below, seen, jnp.where(lane == sub + 8 * q, 1.0, 0.0))
        binv_ref[at, :] = rows[q] * scale_ref[at, :]


def exchange_kernel(
    pivots, matrix, tile_ref, held, returning_ref, right, top, tab_ref,
    incoming_ref, packed_ref, rows_ref, other, linv_ref, upper_ref, scale_ref, pivots_v, pivots_sm, tab_sm,
    arrive, depart, tail_arrive, tail_depart, root_depart, swap_sems, local_sems,
):
    plane, chip = lax.axis_index("prow"), lax.axis_index("pcol")
    rows_dev, cols = matrix.shape
    row_start = plane * rows_dev
    root = chip == 0

    fetch_sm = pltpu.make_async_copy(pivots, pivots_sm, local_sems.at[2])
    fetch_v = pltpu.make_async_copy(pivots, pivots_v, local_sems.at[3])
    fetch_v.start()
    fetch_sm.start()

    @pl.when(root)
    def _():
        for c in range(MOST):
            for t in range(TREES):
                if c < CHUNKS[t]:
                    lo = FIRST[t] + c * PIECE
                    pltpu.make_async_copy(
                        matrix.at[pl.ds(lo, PIECE), pl.ds(0, NB)],
                        held.at[pl.ds(lo, PIECE), :],
                        arrive.at[t, c],
                    ).start()
    load = pltpu.make_async_copy(matrix, tile_ref, local_sems.at[0])
    load.start()

    x, y, z = chip % 4, (chip // 4) % 4, chip // 16
    barrier = pltpu.get_barrier_semaphore()
    for dx, dy, dz in HOPS:
        there = (x + dx) % 4 + 4 * ((y + dy) % 4) + 16 * ((z + dz) % 8)
        pl.semaphore_signal(barrier, inc=1, device_id=(plane, there), device_id_type=MESH)
    pl.semaphore_signal(barrier, inc=1, device_id=(1 - plane, chip), device_id_type=MESH)

    fetch_v.wait()
    pivot_row = jnp.broadcast_to(pivots_v[...], (NB, NB))
    pivot_col = jnp.transpose(pivot_row.astype(F32)).astype(I32)
    swap_lists(pivot_col, pivot_row, row_start, tab_ref)
    move = pltpu.make_async_copy(tab_ref, tab_sm, local_sems.at[1])
    move.start()
    mine = (pivot_col >= row_start) & (pivot_col < row_start + rows_dev)

    def gather_pivots():
        fetch_sm.wait()
        load.wait()

        def some(i, carry):
            for j in range(8):
                k = 8 * i + j
                local = jnp.clip(pivots_sm[0, k] - row_start, 0, rows_dev - 1)
                rows_ref[pl.ds(k, 1), :] = tile_ref[pl.ds(local, 1), :]
            return carry

        lax.fori_loop(0, NB // 8, some, 0)
        swaps[0].start()
        swaps[1].start()

    def swap_of(i, rows, columns):
        return pltpu.make_async_remote_copy(
            src_ref=rows_ref.at[rows, columns], dst_ref=other.at[rows, columns],
            send_sem=swap_sems.at[i, 0], recv_sem=swap_sems.at[i, 1],
            device_id=(1 - plane, chip), device_id_type=MESH,
        )

    swaps = [
        swap_of(0, pl.ds(0, NB), pl.ds(0, NB)),
        swap_of(1, pl.ds(0, NB), pl.ds(NB, cols - NB)),
        swap_of(2, pl.ds(NB, FEW), pl.ds(0, cols)),
    ]

    def gather_displaced():
        move.wait()

        def some(i, carry):
            for j in range(8):
                k = 8 * i + j
                local = jnp.clip(tab_sm[1, k], 0, NB - 1)
                rows_ref[pl.ds(NB + k, 1), :] = tile_ref[pl.ds(local, 1), :]
            return carry

        lax.fori_loop(0, FEW // 8, some, 0)
        swaps[2].start()

    def merge(at):
        incoming_ref[:, at] = jnp.where(mine, rows_ref[:NB, at], other[:NB, at])

    def merge_rest():
        for j in range(1, cols // NB):
            merge(slice(j * NB, (j + 1) * NB))
        returning_ref[...] = jnp.where(plane == 0, rows_ref[NB:, :], other[NB:, :])

    def prepare():
        source = incoming_ref[...]
        lane = lax.broadcasted_iota(I32, (NB, NB), 1)
        sub = lax.broadcasted_iota(I32, (NB, NB), 0)
        packed = packed_ref[...]
        unit = jnp.where(lane < sub, packed, jnp.where(lane == sub, 1.0, 0.0))
        w = jnp.dot(
            held[INV + NB : INV + 2 * NB, :],
            jnp.concatenate([jnp.where(root, -unit, source[:, :NB]), source[:, NB:]], axis=1),
            precision=HIGH, preferred_element_type=F32,
        )
        high = w.astype(BF16)
        right[0:NB, :] = high
        right[NB : 2 * NB, :] = (w - high.astype(F32)).astype(BF16)
        right[2 * NB :, :] = high

        @pl.when(plane == 0)
        def _():
            upper = jnp.dot(
                held[INV : INV + NB, :], source, precision=HIGH, preferred_element_type=F32
            )
            top[...] = jnp.concatenate(
                [jnp.where(root, packed, upper[:, :NB]), upper[:, NB:]], axis=1
            )

    def arrived(at, sem):
        pltpu.make_async_copy(held.at[at, :], held.at[at, :], sem).wait()

    def send(at, out_sem, in_sem, there):
        pltpu.make_async_remote_copy(
            src_ref=held.at[at, :], dst_ref=held.at[at, :], send_sem=out_sem, recv_sem=in_sem,
            device_id=(plane, there), device_id_type=MESH,
        ).start()

    def piece(t, c):
        return pl.ds(pl.multiple_of(FIRST[t] + c * PIECE, 8), PIECE)

    def tail(t):
        return pl.ds(INV + t * TAIL, TAIL)

    def offset(code):
        dx, dy, dz = code % 4, (code // 4) % 4, code // 16
        mirror = (4 - dx) % 4 + 4 * ((4 - dy) % 4) + 16 * ((8 - dz) % 8)
        return jnp.where(plane == 0, code, mirror)

    def steps(word):
        return [(word // 128**i) % 128 for i in range(FAN)]

    @pl.when(root)
    def _():
        def spread(c, trees=range(TREES)):
            for t in trees:
                at = piece(t, c)
                for i, code in enumerate(PANEL_ROOT[t]):
                    send(at, root_depart.at[t, i], arrive.at[t, c], offset(code))

        def staged(c):
            for t in range(TREES):
                if c < CHUNKS[t]:
                    arrived(piece(t, c), arrive.at[t, c])

        pl.semaphore_wait(barrier, len(HOPS) + 1)
        for c in range(SOON):
            staged(c)
            spread(c)
        gather_pivots()
        gather_displaced()
        for c in range(SOON, MOST):
            staged(c)
        for c in range(SOON, EARLY):
            spread(c)
        swaps[0].wait()
        merge(slice(0, NB))
        eliminate(
            incoming_ref[:, :NB], packed_ref, linv_ref, held.at[INV + NB : INV + 2 * NB, :],
            upper_ref, scale_ref, CHUNKS[-1] - EARLY, lambda g: spread(g + EARLY),
            lambda: spread(MOST - 1, [t for t in range(TREES) if CHUNKS[t] == MOST]),
        )
        swaps[1].wait()
        swaps[2].wait()
        held[INV : INV + NB, :] = linv_ref[...]

        @pl.when(plane == 1)
        def _():
            held[INV : INV + FEW, :] = other[NB:, :NB]

        if HELD > INV + 2 * NB:
            held[INV + 2 * NB : HELD, :] = jnp.zeros((HELD - INV - 2 * NB, NB), F32)
        for t in range(TAILS):
            for i, code in enumerate(TAIL_ROOT[t]):
                send(tail(t), root_depart.at[TREES + t, i], tail_arrive.at[t], offset(code))
        merge_rest()
        prepare()
        for t in range(TREES + TAILS):
            for i in range(len((PANEL_ROOT + TAIL_ROOT)[t])):
                at = pl.ds(0, CHUNKS[t] * PIECE if t < TREES else TAIL)
                arrived(at, root_depart.at[t, i])

    @pl.when(chip != 0)
    def _():
        place = jnp.where(plane == 0, chip, (4 - x) % 4 + 4 * ((4 - y) % 4) + 16 * ((8 - z) % 8))
        bits = [(place // (2**i)) % 2 == 1 for i in range(7)]

        def chips_of(word):
            codes, there = steps(word), []
            for code in codes:
                dx, dy, dz = code % 4, (code // 4) % 4, code // 16
                sign = 1 - 2 * plane
                there.append(
                    (x + sign * dx + 4) % 4 + 4 * ((y + sign * dy + 4) % 4)
                    + 16 * ((z + sign * dz + 8) % 8)
                )
            return codes, there

        panel = [chips_of(pick(list(table), bits)) for table in PANEL_TREES]
        turn_words = [pick(list(table), bits) for table in TURNS]
        turns = [(turn_words[t // 5] // 64 ** (t % 5)) % 64 for t in range(TREES + TAILS)]
        tails = [chips_of(pick(list(table), bits)) for table in TAIL_TREES]
        pl.semaphore_wait(barrier, len(HOPS) + 1)
        gather_pivots()
        gather_displaced()

        def send_all(node, at, out_sems, in_sem):
            codes, there = node
            send(at, out_sems.at[0], in_sem, there[0])

            @pl.when(codes[1] > 0)
            def _():
                send(at, out_sems.at[1], in_sem, there[1])

                @pl.when(codes[2] > 0)
                def _():
                    send(at, out_sems.at[2], in_sem, there[2])

                    @pl.when(codes[3] > 0)
                    def _():
                        send(at, out_sems.at[3], in_sem, there[3])

        def pass_on(s, carry):
            for t in range(TREES):
                c = s - turns[t]

                @pl.when((c >= 0) & (c < CHUNKS[t]) & (panel[t][0][0] > 0))
                def _():
                    at = piece(t, c)
                    arrived(at, arrive.at[t, c])
                    send_all(panel[t], at, depart.at[t], arrive.at[t, c])
            for t in range(TAILS):
                @pl.when((turns[TREES + t] == s) & (tails[t][0][0] > 0))
                def _():
                    arrived(tail(t), tail_arrive.at[t])
                    send_all(tails[t], tail(t), tail_depart.at[t], tail_arrive.at[t])
            return carry

        lax.fori_loop(1, max(SPREAD + MOST, TAIL_SPREAD + 1), pass_on, 0)
        for swap in swaps:
            swap.wait()
        merge(slice(0, NB))
        merge_rest()

        for t in range(TAILS):
            @pl.when(tails[t][0][0] == 0)
            def _():
                arrived(tail(t), tail_arrive.at[t])
        prepare()
        for t in range(TREES):
            @pl.when(panel[t][0][0] == 0)
            def _():
                for c in range(CHUNKS[t]):
                    arrived(piece(t, c), arrive.at[t, c])
        for t in range(TREES + TAILS):
            codes = (panel + tails)[t][0]
            for i in range(FAN):
                @pl.when(codes[i] > 0)
                def _():
                    if t < TREES:
                        arrived(pl.ds(0, CHUNKS[t] * PIECE), depart.at[t, i])
                    else:
                        arrived(pl.ds(0, TAIL), tail_depart.at[t - TREES, i])


def exchange(matrix, pivot_rows):
    rows, cols = matrix.shape
    vmem = pl.BlockSpec(memory_space=pltpu.VMEM)
    return pl.pallas_call(
        exchange_kernel,
        name="exchange",
        out_shape=(
            jax.ShapeDtypeStruct((rows, cols), F32),
            jax.ShapeDtypeStruct((HELD, NB), F32),
            jax.ShapeDtypeStruct((FEW, cols), F32),
            jax.ShapeDtypeStruct((3 * NB, cols), BF16),
            jax.ShapeDtypeStruct((NB, cols), F32),
            jax.ShapeDtypeStruct((8, NB), I32),
        ),
        in_specs=[pl.BlockSpec(memory_space=pltpu.HBM)] * 2,
        out_specs=(vmem,) * 6,
        scratch_shapes=[
            pltpu.VMEM((NB, cols), F32),
            pltpu.VMEM((NB, NB), F32),
            pltpu.VMEM((NB + FEW, cols), F32),
            pltpu.VMEM((NB + FEW, cols), F32),
            pltpu.VMEM((NB, NB), F32),
            pltpu.VMEM((NB, NB), F32),
            pltpu.VMEM((NB, NB), F32),
            pltpu.VMEM((1, NB), I32),
            pltpu.SMEM((1, NB), I32),
            pltpu.SMEM((8, NB), I32),
            pltpu.SemaphoreType.DMA((TREES, MOST)),
            pltpu.SemaphoreType.DMA((TREES, FAN)),
            pltpu.SemaphoreType.DMA((TAILS,)),
            pltpu.SemaphoreType.DMA((TAILS, FAN)),
            pltpu.SemaphoreType.DMA((TREES + TAILS, max(map(len, PANEL_ROOT + TAIL_ROOT)))),
            pltpu.SemaphoreType.DMA((3, 2)),
            pltpu.SemaphoreType.DMA((4,)),
        ],
        compiler_params=pltpu.CompilerParams(
            collective_id=0, has_side_effects=True, vmem_limit_bytes=44 * 2**20
        ),
    )(pivot_rows.reshape(1, NB), matrix)


SLOTS = 3


def update_kernel(
    tab, tile_ref, held, returning_ref, right, top, out_ref, slots, patch, ext, sems,
):
    plane, first = lax.axis_index("prow"), lax.axis_index("pcol") == 0
    rows = tile_ref.shape[0]

    def product(left_f32):
        high = left_f32.astype(BF16)
        low = (left_f32 - high.astype(F32)).astype(BF16)
        return jnp.dot(
            jnp.concatenate([high, high, low], axis=1), right[...], preferred_element_type=F32
        )

    def keep(block):
        return jnp.concatenate([jnp.where(first, 0.0, block[:, :NB]), block[:, NB:]], axis=1)

    @pl.when(plane == 1)
    def _():
        ext[...] = held[INV : INV + FEW, :]

    @pl.when(plane == 0)
    def _():
        def take(i, carry):
            for k in range(8):
                row = jnp.clip(tab[1, 8 * i + k], 0, NB - 1)
                ext[pl.ds(8 * i + k, 1), :] = held[pl.ds(row, 1), :]
            return carry

        lax.fori_loop(0, FEW // 8, take, 0)

    patch[...] = keep(returning_ref[...]) - product(ext[...])

    copies = []
    for j in range(rows // TILE):
        slot = slots.at[j % SLOTS]
        if j >= SLOTS:
            copies[j - SLOTS].wait()
        at = slice(j * TILE, (j + 1) * TILE)
        slot[...] = keep(tile_ref[at, :]) - product(held[at, :])
        if j == 0:
            @pl.when(plane == 0)
            def _():
                slot[0:NB, :] = top[...]
        base = plane * rows + j * TILE

        def land(i, carry):
            slot[pl.ds(tab[0, i] - base, 1), :] = patch[pl.ds(i, 1), :]
            return carry

        lax.fori_loop(tab[2, j], tab[2, j + 1], land, 0)
        copies.append(pltpu.make_async_copy(slot, out_ref.at[at, :], sems.at[j % SLOTS]))
        copies[j].start()
    for copy in copies[-SLOTS:]:
        copy.wait()


def update(tile, held, returning, right, top, tab):
    rows, cols = tile.shape
    vmem = pl.BlockSpec(memory_space=pltpu.VMEM)
    return pl.pallas_call(
        update_kernel,
        name="update",
        out_shape=jax.ShapeDtypeStruct((rows, cols), F32),
        in_specs=[pl.BlockSpec(memory_space=pltpu.SMEM)] + [vmem] * 5,
        out_specs=pl.BlockSpec(memory_space=pltpu.HBM),
        scratch_shapes=[
            pltpu.VMEM((SLOTS, TILE, cols), F32),
            pltpu.VMEM((FEW, cols), F32),
            pltpu.VMEM((FEW, NB), F32),
            pltpu.SemaphoreType.DMA((SLOTS,)),
        ],
        compiler_params=pltpu.CompilerParams(vmem_limit_bytes=24 * 2**20),
    )(tab, tile, held, returning, right, top)


def on_device(matrix, pivot_rows):
    return update(*exchange(matrix, pivot_rows))


def solution(mesh):
    return jax.shard_map(
        on_device, mesh=mesh, in_specs=(P("prow", "pcol"), P()), out_specs=P("prow", "pcol"), check_vma=False
    )
```
